32 devices in a mesh: ops: 4 (over z), sec: 8 (over y, x, core).
Axes of the slice: x: 2, y: 2, z: 4, core: 2. Of those that a mesh axis runs over, the one named last changes fastest.
Arguments:
- wavefunction: float32 [512, 128, 128], P(('ops', 'sec')), may hold values from -6 to 6
- left_sector: int32 [512], P(('ops', 'sec')), may hold values from 0 to 15, as said below
- right_sector: int32 [512], P(('ops', 'sec')), may hold values from 0 to 1
- left_size: int32 [16], replicated, may hold values from 64 to 128
- right_size: int32 [2], replicated, may hold values from 64 to 128
- left_ops: float32 [16, 4, 128, 128], P('sec', 'ops'), may hold values from -0.25 to 0.25
- right_ops: float32 [2, 4, 128, 128], P(None, 'ops'), may hold values from -0.5 to 0.5
Outputs:
- sigma: float32 [512, 128, 128], P(('ops', 'sec'))
The draws below stay inside these ranges and needn't reach their ends.
Inputs may be any that keep to these rules, and one draw needn't show every extreme that they name: `left_sector`: the left sectors of the 16 blocks of one device are distinct and come in whole groups g * 2 to g * 2 + 1.
All inputs are finite; a program needn't handle non-finite values.
Results may differ from the reference program's by a relative error of at most 0.0003.
Values sent between devices are 32-bit elements; how exact they have to be, the bound alone decides.
A program may use at most 64 MiB of HBM per device.

```python
import jax
import jax.numpy as jnp
from jax import lax

W = 128
PAIR_DEV = 16
SEC_DEV = 2
RSECT = 2
TERMS = 4
LSECT = 16
BLOCKS = 512
N_OPS = 4
N_SEC = 8


def draw_left_sector(key, part):
    device_count = N_OPS * N_SEC
    group_count = PAIR_DEV // SEC_DEV
    popular = jax.random.randint(jax.random.fold_in(key, 11), (N_SEC,), 0, 1024)
    noise = jax.random.randint(jax.random.fold_in(key, 12), (device_count, N_SEC), 0, 1024)
    scores = (popular[None, :] + noise) * N_SEC + jnp.arange(N_SEC)[None, :]
    chosen = lax.top_k(scores, group_count)[1]
    sectors = chosen[:, :, None] * SEC_DEV + jnp.arange(SEC_DEV)[None, None, :]
    sectors = sectors.reshape(device_count, PAIR_DEV)
    shuffle = jax.random.randint(jax.random.fold_in(key, 13), (device_count, PAIR_DEV), 0, 65536) * PAIR_DEV + jnp.arange(PAIR_DEV)[None, :]
    order = jnp.argsort(shuffle, axis=1)
    return jnp.take_along_axis(sectors, order, axis=1).reshape(device_count * PAIR_DEV).astype(jnp.int32)


def place_ends(array, rng, low, largest):
    dims = array.shape
    place = [jax.random.randint(jax.random.fold_in(rng, axis), (), 0, dims[axis]) for axis in range(len(dims))]
    array = array.at[tuple(place)].set(low)
    longest = dims.index(max(dims))
    place[longest] = (place[longest] + 1) % dims[longest]
    return array.at[tuple(place)].set(largest)


def level_of(rng, extent, split, least, top_value):
    gain, own = 1.0, jax.random.fold_in(rng, 6)
    for dim, blocks in split:
        draws = jnp.exp(jax.random.uniform(jax.random.fold_in(own, dim), (blocks,), jnp.float32, least / len(split), top_value / len(split)))
        gain = gain * jnp.repeat(draws, extent[dim] // blocks).reshape([-1 if axis == dim else 1 for axis in range(len(extent))])
    return gain


def gaussian(own_key, shape, spread, reach, shards=(), kind=jnp.bfloat16):
    entries = jax.random.normal(own_key, shape, jnp.float32) * spread
    if len(shards) > 0:
        entries = level_of(own_key, shape, shards, -0.22, 0.18) * entries
    return jnp.clip(entries, min=-reach, max=reach).astype(kind)


def setup_inputs(seed: int = 0) -> dict:
    key_list = jax.random.split(jax.random.key(seed), 8)
    return {
        "wavefunction": gaussian(key_list[0], (BLOCKS, W, W), 1.0, 6.0, ((0, 32),), jnp.float32),
        "left_sector": draw_left_sector(jax.random.fold_in(key_list[7], 71), 0),
        "right_sector": place_ends(jax.random.randint(key_list[2], (BLOCKS,), 0, RSECT), jax.random.fold_in(key_list[2], 1), 0, RSECT - 1).astype(jnp.int32),
        "left_size": place_ends(jax.random.randint(key_list[3], (LSECT,), W // 2, W + 1), jax.random.fold_in(key_list[3], 1), W // 2, W).astype(jnp.int32),
        "right_size": jax.random.randint(key_list[4], (RSECT,), W // 2, W + 1).astype(jnp.int32),
        "left_ops": gaussian(key_list[5], (LSECT, TERMS, W, W), (W * TERMS) ** -0.5, 0.25, ((0, 8), (1, 4)), jnp.float32),
        "right_ops": gaussian(key_list[6], (RSECT, TERMS, W, W), W ** -0.5, 0.5, ((1, 4),), jnp.float32),
    }


def reference(wavefunction, left_sector, right_sector, left_size, right_size, left_ops, right_ops):
    position = jnp.arange(W)

    def single(inputs):
        block, left_id, right_id = inputs
        row_live = position < left_size[left_id]
        col_live = position < right_size[right_id]
        window = (row_live[:, None] & col_live[None, :]).astype(jnp.float32)
        masked = block * window
        left_pick = left_ops[left_id]
        right_pick = right_ops[right_id]
        halfway = jnp.einsum('ij,tlj->til', masked, right_pick, precision=lax.Precision.HIGHEST)
        result = jnp.einsum('tmi,til->ml', left_pick, halfway, precision=lax.Precision.HIGHEST)
        return result * window

    return lax.map(single, (wavefunction, left_sector, right_sector))
```

```python
import jax
import jax.numpy as jnp
from jax import lax
from jax.experimental import pallas as pl
from jax.experimental.pallas import tpu as pltpu
from jax.sharding import PartitionSpec as P

MESH = pl.DeviceIdType.MESH


def contract(running, packed, left_ids, right_ids, live_count, left_blocks, right_blocks):
    turn_count = (live_count + 1) // 2

    def advance(turn_index, current):
        first = 2 * turn_index
        block = lax.dynamic_slice_in_dim(packed, first, 2, 0)
        left_sel = lax.dynamic_slice_in_dim(left_ids, first, 2, 0)
        right_sel = lax.dynamic_slice_in_dim(right_ids, first, 2, 0)
        left_pick = left_blocks[left_sel]
        right_pick = right_blocks[right_sel]
        halfway = jnp.einsum("sij,stlj->stil", block, right_pick, precision=lax.Precision.HIGHEST)
        update = jnp.einsum("stmi,stil->sml", left_pick, halfway, precision=lax.Precision.HIGHEST)
        before = lax.dynamic_slice_in_dim(current, first, 2, 0)
        return lax.dynamic_update_slice_in_dim(current, before + update, first, 0)

    return lax.fori_loop(0, turn_count, advance, running)


def gather_whole(left_ops, right_ops):
    return (
        lax.all_gather(left_ops, "ops", axis=1, tiled=True),
        lax.all_gather(right_ops, "ops", axis=1, tiled=True),
    )


def arrange(incoming, tags, slot_count, width):
    incoming = incoming.reshape(slot_count, width, width)
    tag_ids = tags.reshape(slot_count).astype(jnp.int32)
    live_flag = (tag_ids > 0).astype(jnp.int32)
    order = jnp.argsort(1 - live_flag, stable=True)
    live_count = jnp.sum(live_flag)
    packed = incoming[order]
    right_ids = jnp.maximum(tag_ids[order] - 1, 0)
    return (packed, right_ids, order, live_count)


def shards(wavefunction, left_sector, right_sector, left_size, right_size, left_ops, right_ops):
    peer_count = lax.axis_size("sec")
    sec_local = left_ops.shape[0]
    width = wavefunction.shape[1]
    position = jnp.arange(width)
    left_live = jnp.sum(
        jnp.where(
            left_sector[:, None] == jnp.arange(left_size.shape[0])[None, :], left_size[None, :], 0
        ),
        axis=1,
    )
    right_live = jnp.sum(
        jnp.where(
            right_sector[:, None] == jnp.arange(right_size.shape[0])[None, :],
            right_size[None, :],
            0,
        ),
        axis=1,
    )
    row_live = position[None, :] < left_live[:, None]
    col_live = position[None, :] < right_live[:, None]
    window = (row_live[:, :, None] & col_live[:, None, :]).astype(jnp.float32)
    masked = wavefunction * window
    owner = left_sector // sec_local
    within = left_sector % sec_local
    outgoing = (
        jnp.zeros((peer_count, sec_local, width, width), jnp.float32).at[owner, within].set(masked)
    )
    labels = (
        jnp.zeros((peer_count, sec_local), jnp.float32)
        .at[owner, within]
        .set((right_sector + 1).astype(jnp.float32))
    )
    incoming, tags = (
        lax.all_to_all(outgoing, "sec", split_axis=0, concat_axis=0, tiled=True),
        lax.all_to_all(labels, "sec", split_axis=0, concat_axis=0, tiled=True),
    )
    slot_count = peer_count * sec_local
    packed, right_ids, order, live_count = arrange(incoming, tags, slot_count, width)
    left_ids = order % sec_local
    empty = jnp.zeros_like(packed)
    left_all, right_all = gather_whole(left_ops, right_ops)
    result = contract(empty, packed, left_ids, right_ids, live_count, left_all, right_all)
    restored = jnp.zeros_like(result).at[order].set(result)
    returned = lax.all_to_all(
        restored.reshape(peer_count, sec_local, width, width),
        "sec",
        split_axis=0,
        concat_axis=0,
        tiled=True,
    )
    return returned[owner, within] * window


def term_orders(count):
    orders = []
    for here in range(count):
        orders.append(sorted(range(count), key=lambda t: (abs(t - here), abs(2 * t - count + 1), t)))
    return orders


def split(value):
    high = value.astype(jnp.bfloat16)
    low = (value - high.astype(jnp.float32)).astype(jnp.bfloat16)
    return high, low


def gather_contract(
    wf_hbm, lops_hbm, rops_hbm, lsec, rsec, lsize, rsize,
    out_ref,
    out_sem, wbuf, lbuf, rbuf, mcat, hcat, acc, inverse, right_of,
    own_sem, recv_l, recv_r, send_x, send_y, send_up, send_dn, send_sib,
):
    terms = lax.axis_size("ops")
    sectors, _, width, _ = lbuf.shape
    rights = rbuf.shape[1]
    half = width // 2
    z = lax.axis_index("ops")
    sec = lax.axis_index("sec")
    core = sec % 2
    xpos = (sec // 2) % 2
    ypos = sec // 4
    sib = sec + 1 - 2 * core
    xnb = sec + 2 - 4 * xpos
    ynb = sec + 4 - 8 * ypos
    dnb = xnb + 4 - 8 * ypos
    has_up = z < terms - 1
    has_dn = z > 0
    table = term_orders(terms)
    order = []
    for k in range(terms):
        value = table[0][k] * 1
        for here in range(1, terms):
            value = jnp.where(z == here, table[here][k], value)
        order.append(value)

    def flip(group):
        return group + 1 - 2 * core

    barrier = pltpu.get_barrier_semaphore()

    def greet(zz, ss):
        pl.semaphore_signal(barrier, inc=1, device_id=(zz, ss), device_id_type=MESH)

    for peer in (sib, xnb, ynb):
        greet(z, peer)

    @pl.when(has_up)
    def _():
        greet(z + 1, sec)

    @pl.when(has_dn)
    def _():
        greet(z - 1, sec)

    own_l = [
        pltpu.make_async_copy(lops_hbm.at[i, 0], lbuf.at[2 * sec + i, z], recv_l.at[2 * sec + i, z])
        for i in range(2)
    ]
    own_r = pltpu.make_async_copy(rops_hbm.at[:, 0], rbuf.at[z], own_sem.at[0])
    own_w = pltpu.make_async_copy(wf_hbm, wbuf, own_sem.at[1])
    own_w.start()
    own_r.start()
    for copy in own_l:
        copy.start()
    pl.semaphore_wait(barrier, 3 + has_up.astype(jnp.int32) + has_dn.astype(jnp.int32))

    def move(src, dst, ssem, rsem, zz, ss):
        return pltpu.make_async_remote_copy(
            src_ref=src, dst_ref=dst, send_sem=ssem, recv_sem=rsem,
            device_id=(zz, ss), device_id_type=MESH,
        )

    def piece(group, i, t, ssem, zz, ss, own=False):
        s = 2 * group + i
        src = lops_hbm.at[i, 0] if own else lbuf.at[s, t]
        return move(src, lbuf.at[s, t], ssem, recv_l.at[s, t], zz, ss)

    def rpiece(h, t, ssem, zz, ss, own=False):
        rows = pl.ds(pl.multiple_of(h * half, half), half)
        src = rops_hbm.at[:, 0, rows] if own else rbuf.at[t, :, rows]
        return move(src, rbuf.at[t, :, rows], ssem, recv_r.at[t, h], zz, ss)

    def await_l(group, i, t):
        piece(group, i, t, send_x.at[t, 0], z, xnb).wait_recv()

    def await_r(h, t):
        rpiece(h, t, send_x.at[t, 0], z, xnb).wait_recv()

    def along(make, j, t, own, act):
        up = has_up & (t <= z)
        dn = has_dn & (t >= z)

        @pl.when(up)
        def _():
            act(make(t, send_up.at[t, j], z + 1, sec, own))

        @pl.when(dn)
        def _():
            act(make(t, send_dn.at[t, j], z - 1, sec, own))

    def fan_own(i, t, own, act):
        along(lambda t, ssem, zz, ss, own: piece(sec, i, t, ssem, zz, ss, own), i, t, own, act)
        act(piece(sec, i, t, send_x.at[t, i], z, xnb, own))
        act(piece(sec, i, t, send_y.at[t, i], z, ynb, own))
        act(piece(sec, i, t, send_sib.at[t, i], z, sib, own))

    def fan_right(t, own, act):
        along(lambda t, ssem, zz, ss, own: rpiece(core, t, ssem, zz, ss, own), 2, t, own, act)
        if not own:
            act(rpiece(core, t, send_sib.at[t, 8], z, sib))

    def fan_x(i, t, act):
        if i == 0:
            act(piece(xnb, i, t, send_y.at[t, 2], z, ynb))
        act(piece(xnb, i, t, send_sib.at[t, 2 + i], z, sib))

    def fan_y(i, t, act):
        if i == 1:
            act(piece(ynb, i, t, send_x.at[t, 2], z, xnb))
        act(piece(ynb, i, t, send_sib.at[t, 4 + i], z, sib))

    def fan_d(i, t, act):
        act(piece(dnb, i, t, send_sib.at[t, 6 + i], z, sib))

    start = lambda copy: copy.start()
    drain = lambda copy: copy.wait_send()

    t0 = order[0]
    for i in range(2):
        fan_own(i, t0, True, start)
    fan_right(t0, True, start)

    for s in range(sectors):
        value = jnp.int32(0)
        for p in range(1, sectors):
            value = jnp.where(lsec[p] == s, p, value)
        inverse[s] = value
        right_of[s] = rsec[value]

    row_at = lax.broadcasted_iota(jnp.int32, (width, width), 0)
    col_at = lax.broadcasted_iota(jnp.int32, (width, width), 1)

    own_w.wait()

    @pl.loop(0, sectors)
    def _(s):
        live = (row_at < lsize[s]) & (col_at < rsize[right_of[s]])
        high, low = split(jnp.where(live, wbuf[inverse[s]], 0.0))
        rows = pl.ds(pl.multiple_of(s * width, width), width)
        mcat[rows, :width] = high
        mcat[rows, width:] = low
        acc[s] = jnp.zeros((width, width), jnp.float32)

    own_r.wait()
    batch = 4 if sectors % 4 == 0 else 1

    def halfway(t):
        high, low = split(rbuf[t].reshape(rights * width, width))
        doubled = jnp.concatenate([high, high], axis=1)
        contract_last = (((1,), (1,)), ((), ()))

        @pl.loop(0, sectors // batch)
        def _(n):
            rows = pl.ds(pl.multiple_of(n * batch * width, batch * width), batch * width)
            left = mcat[rows, :]
            both = lax.dot_general(left, doubled, contract_last, preferred_element_type=jnp.float32)
            both += lax.dot_general(
                left[:, :width], low, contract_last, preferred_element_type=jnp.float32
            )
            for j in range(batch):
                s = n * batch + j
                mine = both[j * width : (j + 1) * width]
                which = jnp.full((width, width), right_of[s], jnp.int32)
                pick = mine[:, :width]
                for b in range(1, rights):
                    pick = jnp.where(which == b, mine[:, b * width : (b + 1) * width], pick)
                h_high, h_low = split(pick)
                hcat[t, s, :, :width] = h_high
                hcat[t, s, :, width:] = h_low

    def apply_left(s, t):
        high, low = split(lbuf[s, t])
        wide = jnp.dot(
            jnp.concatenate([high, low], axis=0), hcat[t, s], preferred_element_type=jnp.float32
        )
        acc[s] += wide[:width, :width] + (wide[:width, width:] + wide[width:, :width])

    def apply_group(group, t, wait):
        if wait:
            for i in range(2):
                await_l(group, i, t)
        for i in range(2):
            apply_left(2 * group + i, t)

    def land_own(k, i):
        await_l(sec, i, order[k])
        fan_own(i, order[k], False, start)

    def land_side(k, i):
        await_l(xnb, i, order[k])
        fan_x(i, order[k], start)
        await_l(ynb, i, order[k])
        fan_y(i, order[k], start)

    def land_far(k):
        for i in range(2):
            await_l(dnb, i, order[k])
            fan_d(i, order[k], start)

    def land_right(k):
        await_r(core, order[k])
        fan_right(order[k], False, start)

    def apply_side(k):
        apply_group(xnb, order[k], False)
        apply_group(ynb, order[k], False)
        apply_group(flip(xnb), order[k], True)
        apply_group(flip(ynb), order[k], True)

    def apply_far(k):
        apply_group(dnb, order[k], False)
        apply_group(flip(dnb), order[k], True)

    def apply_own(k):
        await_r(1 - core, order[k])
        halfway(order[k])
        apply_group(sec, order[k], False)
        apply_group(sib, order[k], True)

    middle = has_up & has_dn
    border = jnp.logical_not(middle)

    for copy in own_l:
        copy.wait()
    halfway(order[0])
    apply_group(sec, order[0], False)

    for i in range(2):
        land_own(1, i)
        land_side(0, i)

    @pl.when(middle)
    def _():
        for i in range(2):
            land_own(2, i)

    apply_group(sib, order[0], True)
    apply_side(0)
    land_right(1)
    land_side(1, 0)
    apply_own(1)
    land_side(1, 1)

    @pl.when(border)
    def _():
        for i in range(2):
            land_own(2, i)

    @pl.when(middle)
    def _():
        for i in range(2):
            land_own(3, i)
        land_right(2)

    land_far(0)
    apply_side(1)

    @pl.when(border)
    def _():
        for i in range(2):
            land_own(3, i)

    @pl.when(middle)
    def _():
        land_right(3)

    for i in range(2):
        land_side(2, i)
    apply_far(0)

    @pl.when(border)
    def _():
        land_right(2)

    apply_own(2)
    for i in range(2):
        land_side(3, i)
    apply_side(2)

    @pl.when(border)
    def _():
        land_right(3)

    land_far(1)
    apply_own(3)
    apply_far(1)
    land_far(2)
    apply_side(3)
    land_far(3)
    apply_far(2)
    apply_far(3)

    for p in range(sectors):
        s = lsec[p]
        live = (row_at < lsize[s]) & (col_at < rsize[rsec[p]])
        out_ref[p] = jnp.where(live, acc[s], 0.0)

    for k in range(terms):
        t = order[k]
        for i in range(2):
            fan_own(i, t, k == 0, drain)
            fan_x(i, t, drain)
            fan_y(i, t, drain)
            fan_d(i, t, drain)
        fan_right(t, k == 0, drain)


def local_shards(wavefunction, left_sector, right_sector, left_size, right_size, left_ops, right_ops):
    terms = lax.axis_size("ops")
    sectors, width = left_size.shape[0], wavefunction.shape[1]
    rights = right_size.shape[0]
    dma = pltpu.SemaphoreType.DMA
    anywhere = pl.BlockSpec(memory_space=pl.ANY)
    scalars = pl.BlockSpec(memory_space=pltpu.SMEM)
    return pl.pallas_call(
        gather_contract,
        out_shape=pltpu.VMEM(wavefunction.shape, jnp.float32),
        in_specs=[pl.BlockSpec(memory_space=pltpu.HBM)] * 3 + [scalars] * 4,
        out_specs=pl.BlockSpec(memory_space=pltpu.VMEM),
        scratch_shapes=[
            dma((sectors,)),
            pltpu.VMEM(wavefunction.shape, jnp.float32),
            pltpu.VMEM((sectors, terms, width, width), jnp.float32),
            pltpu.VMEM((terms, rights, width, width), jnp.float32),
            pltpu.VMEM((sectors * width, 2 * width), jnp.bfloat16),
            pltpu.VMEM((terms, sectors, width, 2 * width), jnp.bfloat16),
            pltpu.VMEM((sectors, width, width), jnp.float32),
            pltpu.SMEM((sectors,), jnp.int32),
            pltpu.SMEM((sectors,), jnp.int32),
            dma((2,)),
            dma((sectors, terms)),
            dma((terms, 2)),
            dma((terms, 3)),
            dma((terms, 3)),
            dma((terms, 3)),
            dma((terms, 3)),
            dma((terms, 9)),
        ],
        compiler_params=pltpu.CompilerParams(collective_id=0, has_side_effects=True, vmem_limit_bytes=40*2**20),
    )(*[pltpu.with_memory_space_constraint(a, pltpu.HBM) for a in (wavefunction, left_ops, right_ops, left_sector, right_sector, left_size, right_size)])


def cube_shards(*arrays):
    wavefunction, left_size, left_ops = arrays[0], arrays[3], arrays[5]
    sectors, width = left_size.shape[0], wavefunction.shape[1]
    terms = lax.axis_size("ops")
    every_sector = wavefunction.shape[0] == sectors
    cube = lax.axis_size("sec") == 2**3 and terms == 2**2 and left_ops.shape[:2] == (2, 1)
    small = sectors * terms * width * width * 4 <= 2**23
    if every_sector and cube and small:
        return local_shards(*arrays)
    return shards(*arrays)


def solution(mesh):
    placed = (
        P(("ops", "sec"), None, None),
        P(("ops", "sec")),
        P(("ops", "sec")),
        P(),
        P(),
        P("sec", "ops", None, None),
        P(None, "ops", None, None),
    )
    return jax.shard_map(
        cube_shards, mesh=mesh, in_specs=placed, out_specs=P(("ops", "sec"), None, None), check_vma=False
    )
```

```python
import jax
import jax.numpy as jnp
from jax import lax
from jax.experimental import pallas as pl
from jax.experimental.pallas import tpu as pltpu
from jax.sharding import PartitionSpec as P

MESH = pl.DeviceIdType.MESH


def contract(running, packed, left_ids, right_ids, live_count, left_blocks, right_blocks):
    turn_count = (live_count + 1) // 2

    def advance(turn_index, current):
        first = 2 * turn_index
        block = lax.dynamic_slice_in_dim(packed, first, 2, 0)
        left_sel = lax.dynamic_slice_in_dim(left_ids, first, 2, 0)
        right_sel = lax.dynamic_slice_in_dim(right_ids, first, 2, 0)
        left_pick = left_blocks[left_sel]
        right_pick = right_blocks[right_sel]
        halfway = jnp.einsum("sij,stlj->stil", block, right_pick, precision=lax.Precision.HIGHEST)
        update = jnp.einsum("stmi,stil->sml", left_pick, halfway, precision=lax.Precision.HIGHEST)
        before = lax.dynamic_slice_in_dim(current, first, 2, 0)
        return lax.dynamic_update_slice_in_dim(current, before + update, first, 0)

    return lax.fori_loop(0, turn_count, advance, running)


def gather_whole(left_ops, right_ops):
    return (
        lax.all_gather(left_ops, "ops", axis=1, tiled=True),
        lax.all_gather(right_ops, "ops", axis=1, tiled=True),
    )


def arrange(incoming, tags, slot_count, width):
    incoming = incoming.reshape(slot_count, width, width)
    tag_ids = tags.reshape(slot_count).astype(jnp.int32)
    live_flag = (tag_ids > 0).astype(jnp.int32)
    order = jnp.argsort(1 - live_flag, stable=True)
    live_count = jnp.sum(live_flag)
    packed = incoming[order]
    right_ids = jnp.maximum(tag_ids[order] - 1, 0)
    return (packed, right_ids, order, live_count)


def shards(wavefunction, left_sector, right_sector, left_size, right_size, left_ops, right_ops):
    peer_count = lax.axis_size("sec")
    sec_local = left_ops.shape[0]
    width = wavefunction.shape[1]
    position = jnp.arange(width)
    left_live = jnp.sum(
        jnp.where(
            left_sector[:, None] == jnp.arange(left_size.shape[0])[None, :], left_size[None, :], 0
        ),
        axis=1,
    )
    right_live = jnp.sum(
        jnp.where(
            right_sector[:, None] == jnp.arange(right_size.shape[0])[None, :],
            right_size[None, :],
            0,
        ),
        axis=1,
    )
    row_live = position[None, :] < left_live[:, None]
    col_live = position[None, :] < right_live[:, None]
    window = (row_live[:, :, None] & col_live[:, None, :]).astype(jnp.float32)
    masked = wavefunction * window
    owner = left_sector // sec_local
    within = left_sector % sec_local
    outgoing = (
        jnp.zeros((peer_count, sec_local, width, width), jnp.float32).at[owner, within].set(masked)
    )
    labels = (
        jnp.zeros((peer_count, sec_local), jnp.float32)
        .at[owner, within]
        .set((right_sector + 1).astype(jnp.float32))
    )
    incoming, tags = (
        lax.all_to_all(outgoing, "sec", split_axis=0, concat_axis=0, tiled=True),
        lax.all_to_all(labels, "sec", split_axis=0, concat_axis=0, tiled=True),
    )
    slot_count = peer_count * sec_local
    packed, right_ids, order, live_count = arrange(incoming, tags, slot_count, width)
    left_ids = order % sec_local
    empty = jnp.zeros_like(packed)
    left_all, right_all = gather_whole(left_ops, right_ops)
    result = contract(empty, packed, left_ids, right_ids, live_count, left_all, right_all)
    restored = jnp.zeros_like(result).at[order].set(result)
    returned = lax.all_to_all(
        restored.reshape(peer_count, sec_local, width, width),
        "sec",
        split_axis=0,
        concat_axis=0,
        tiled=True,
    )
    return returned[owner, within] * window


def split(value):
    high = value.astype(jnp.bfloat16)
    low = (value - high.astype(jnp.float32)).astype(jnp.bfloat16)
    return high, low


LAND, SIBLING, ALONG_X, ALONG_Y, ALONG_UP, ALONG_DOWN, RIGHTS, LEFT, SIBLING_LEFT, LAND_SIBLING = range(10)

PROGRAMS = (
    (
        600, 8, 20, 220, 308, 610, 708, 108, 1, 201, 16, 5, 305, 704, 301, 120,
        101, 205, 700, 41, 900, 800, 24, 424, 116, 28, 2, 202, 141, 302, 128, 21,
        221, 9, 428, 102, 12, 6, 109, 306, 601, 720, 121, 105, 17, 206, 117, 309,
        611, 724, 112, 916, 42, 13, 142, 712, 716, 10, 901, 18, 705, 310, 3, 203,
        110, 303, 602, 103, 113, 124, 22, 222, 612, 709, 801, 701, 29, 7, 118, 107,
        106, 717, 718, 25, 702, 710, 207, 307, 122, 14, 129, 917, 817, 43, 143, 722,
        804, 805, 714, 821, 729, 11, 908, 26, 125, 111, 902, 909, 809, 603, 613, 812,
        820, 813, 126, 114, 19, 903, 924, 828, 30, 130, 119, 925, 807, 703, 707, 726,
        806, 730, 803, 706, 728, 816, 802, 713, 824, 27, 127, 15, 910, 810, 918, 818,
        115, 23, 123, 822, 723, 721, 715, 725, 825, 31, 131, 829, 711, 808, 911, 811,
        926, 919, 727, 830, 731, 826, 719, 815, 814, 819, 823, 927, 827, 831,
    ),
    (
        2, 0, 202, 21, 300, 502, 302, 4, 102, 304, 6, 506, 404, 221, 17, 117,
        400, 601, 611, 42, 306, 204, 40, 206, 9, 140, 542, 440, 121, 309, 3, 16,
        203, 503, 10, 142, 600, 103, 310, 116, 18, 7, 106, 507, 109, 610, 602, 104,
        24, 20, 424, 43, 200, 120, 29, 207, 543, 303, 12, 143, 901, 22, 705, 13,
        110, 28, 428, 612, 702, 603, 118, 25, 129, 112, 107, 805, 125, 801, 14, 222,
        11, 307, 113, 710, 122, 100, 27, 527, 124, 26, 613, 8, 108, 114, 720, 916,
        31, 531, 15, 131, 19, 128, 918, 127, 707, 727, 716, 818, 709, 119, 111, 126,
        708, 822, 703, 724, 717, 711, 820, 917, 817, 23, 123, 816, 115, 30, 130, 909,
        927, 903, 910, 810, 731, 706, 725, 919, 803, 911, 813, 704, 718, 807, 719, 821,
        730, 729, 809, 924, 908, 808, 714, 819, 721, 713, 925, 829, 926, 900, 800, 902,
        806, 828, 814, 700, 831, 815, 812, 824, 715, 826, 701, 723, 827, 830, 726, 728,
        823, 804, 802, 811, 712, 825, 722,
    ),
    (
        3, 503, 303, 203, 602, 612, 10, 110, 103, 1, 5, 405, 7, 18, 305, 201,
        507, 401, 43, 105, 301, 205, 41, 118, 143, 441, 543, 22, 107, 11, 222, 207,
        111, 19, 307, 141, 4, 310, 404, 603, 601, 21, 9, 613, 0, 300, 119, 122,
        903, 221, 200, 104, 400, 14, 13, 27, 527, 309, 204, 121, 304, 113, 702, 40,
        127, 440, 114, 17, 30, 31, 531, 23, 140, 123, 902, 611, 731, 15, 130, 109,
        131, 26, 126, 600, 719, 24, 124, 117, 100, 910, 810, 918, 424, 803, 16, 28,
        101, 116, 726, 610, 716, 428, 8, 25, 901, 29, 115, 806, 728, 703, 927, 707,
        706, 714, 108, 919, 819, 900, 128, 704, 717, 831, 804, 722, 710, 20, 125, 917,
        817, 12, 721, 713, 821, 718, 112, 911, 926, 120, 924, 827, 705, 802, 805, 814,
        708, 129, 909, 813, 709, 818, 725, 727, 720, 724, 715, 908, 800, 826, 730, 808,
        809, 723, 916, 816, 801, 701, 820, 811, 925, 825, 829, 824, 830, 823, 712, 807,
        729, 815, 711, 812, 700, 828, 822,
    ),
    (
        603, 11, 311, 23, 223, 613, 2, 6, 202, 19, 123, 206, 111, 106, 306, 42,
        27, 527, 15, 119, 127, 142, 102, 302, 115, 31, 131, 5, 205, 531, 305, 10,
        110, 731, 22, 1, 222, 711, 301, 310, 903, 41, 201, 911, 141, 602, 612, 105,
        101, 14, 4, 13, 204, 927, 719, 304, 21, 601, 611, 703, 815, 121, 0, 701,
        114, 221, 18, 17, 901, 300, 30, 122, 9, 309, 109, 26, 200, 130, 118, 40,
        140, 117, 721, 805, 722, 715, 807, 727, 803, 718, 710, 705, 104, 600, 702, 126,
        20, 120, 113, 610, 24, 12, 910, 112, 917, 821, 100, 124, 29, 926, 830, 817,
        827, 902, 918, 707, 810, 814, 826, 801, 806, 919, 819, 16, 116, 900, 28, 129,
        8, 128, 25, 108, 804, 811, 822, 823, 725, 700, 125, 916, 704, 729, 726, 730,
        800, 816, 723, 728, 820, 724, 712, 818, 924, 824, 720, 717, 802, 925, 909, 908,
        813, 809, 828, 825, 706, 829, 808, 831, 713, 709, 812, 708, 714, 716,
    ),
)


def gather_contract(
    wf_hbm, lops_hbm, rops_hbm, lsec_hbm, rsec_hbm, lsize_hbm, rsize_hbm,
    out_ref,
    wbuf, lbuf, rbuf, mcat, hcat, acc, lsec, rsec, lsize, rsize, inverse, right_of,
    own_sem, recv_own, recv_sib, recv_r, sends, entered,
):
    terms = lax.axis_size("ops")
    sectors, _, width, _ = lbuf.shape
    rights = rbuf.shape[1]
    half = width // 2
    z = lax.axis_index("ops")
    sec = lax.axis_index("sec")
    core = sec % 2
    xpos = (sec // 2) % 2
    ypos = sec // 4
    sib = sec + 1 - 2 * core
    xnb = sec + 2 - 4 * xpos
    ynb = sec + 4 - 8 * ypos
    dnb = xnb + 4 - 8 * ypos
    has_up = z < terms - 1
    has_dn = z > 0

    def flip(group):
        return group + 1 - 2 * core

    barrier = pltpu.get_barrier_semaphore()

    def greet(sem, zz, ss):
        pl.semaphore_signal(sem, inc=1, device_id=(zz, ss), device_id_type=MESH)

    links = (
        (xpos == 0, xpos == 1, z, xnb),
        (ypos == 0, ypos == 1, z, ynb),
        (has_up, has_dn, z, sec),
        (core == 1, core == 0, z, sib),
    )
    for k, (first, second, zz, ss) in enumerate(links):
        @pl.when(first)
        def _(k=k, zz=zz, ss=ss):
            greet(barrier, zz + 1 if k == 2 else zz, ss)

    scalar_in = [
        pltpu.make_async_copy(src, dst, own_sem.at[2 + n])
        for n, (src, dst) in enumerate(
            ((lsec_hbm, lsec), (rsec_hbm, rsec), (lsize_hbm, lsize), (rsize_hbm, rsize))
        )
    ]
    own_l = [
        pltpu.make_async_copy(lops_hbm.at[i, 0], lbuf.at[2 * sec + i, z], recv_own.at[0, i, z])
        for i in range(2)
    ]
    own_r = pltpu.make_async_copy(rops_hbm.at[:, 0], rbuf.at[z], own_sem.at[0])
    own_w = pltpu.make_async_copy(wf_hbm, wbuf, own_sem.at[1])
    for copy in scalar_in:
        copy.start()
    own_w.start()
    own_r.start()
    for copy in own_l:
        copy.start()
    firsts = xpos + ypos + has_dn.astype(jnp.int32) + 1 - core

    @pl.when(firsts > 0)
    def _():
        pl.semaphore_wait(barrier, firsts)

    for k, (first, second, zz, ss) in enumerate(links):
        @pl.when(second)
        def _(k=k, zz=zz, ss=ss):
            greet(entered.at[k], zz - 1 if k == 2 else zz, ss)

    def move(src, dst, ssem, rsem, zz, ss):
        return pltpu.make_async_remote_copy(
            src_ref=src, dst_ref=dst, send_sem=ssem, recv_sem=rsem,
            device_id=(zz, ss), device_id_type=MESH,
        )

    def piece(group, i, t, link, rsem, zz, ss, own=False):
        s = 2 * group + i
        src = lops_hbm.at[i, 0] if own else lbuf.at[s, t]
        return move(src, lbuf.at[s, t], sends.at[link], rsem, zz, ss)

    def rpiece(h, t, link, zz, ss, own=False):
        rows = pl.ds(pl.multiple_of(h * half, half), half)
        src = rops_hbm.at[:, 0, rows] if own else rbuf.at[t, :, rows]
        return move(src, rbuf.at[t, :, rows], sends.at[link], recv_r.at[t, h], zz, ss)

    def await_l(place, i, t):
        group = groups[place]
        piece(group, i, t, 0, recv_own.at[place, i, t], z, xnb).wait_recv()

    def await_pair(place, t):
        first = 2 * flip(groups[place])
        pair = lbuf.at[pl.ds(first, 2), t]
        move(pair, pair, sends.at[0], recv_sib.at[place, t], z, sib).wait_recv()

    def await_r(h, t):
        rpiece(h, t, 0, z, xnb).wait_recv()

    def drain(link, count):
        blocks = wbuf.at[pl.ds(0, count)]
        move(blocks, blocks, sends.at[link], recv_own.at[0, 0, 0], z, xnb).wait_send()

    groups = (sec, xnb, ynb, dnb)
    sides = {ALONG_UP: (2, 1), ALONG_DOWN: (3, -1)}

    def to_z(way, place, i, t, own=False):
        link, step = sides[way]
        return piece(groups[place], i, t, link, recv_own.at[place, i, t], z + step, sec, own)

    def right_z(way, t, own=False):
        link, step = sides[way]
        return rpiece(core, t, link, z + step, sec, own)

    def to_x(place, i, t, own=False):
        return piece(groups[place], i, t, 0, recv_own.at[place + 1, i, t], z, xnb, own)

    def to_y(place, i, t, own=False):
        return piece(groups[place], i, t, 1, recv_own.at[place + 2, i, t], z, ynb, own)

    def to_sib(place, i, t, own=False):
        link = 4 + (place + 1) // 2
        return piece(groups[place], i, t, link, recv_sib.at[place, t], z, sib, own)

    def own_z(way):
        return [to_z(way, 0, 0, z, True), to_z(way, 0, 1, z, True), right_z(way, z, True)]

    own_sends = (
        [to_x(0, 0, z, True), to_x(0, 1, z, True)],
        [to_y(0, 1, z, True), to_y(0, 0, z, True)],
        [to_sib(0, 0, z, True), to_sib(0, 1, z, True)],
    )

    def start(copies):
        for copy in copies:
            copy.start()

    @pl.when(xpos == 1)
    def _():
        start(own_sends[0])

    @pl.when(ypos == 1)
    def _():
        start(own_sends[1])

    @pl.when(has_dn)
    def _():
        start(own_z(ALONG_DOWN))

    @pl.when(core == 0)
    def _():
        start(own_sends[2])

    for copy in scalar_in:
        copy.wait()
    for s in range(sectors):
        value = jnp.int32(0)
        for p in range(1, sectors):
            value = jnp.where(lsec[p] == s, p, value)
        inverse[s] = value
        right_of[s] = rsec[value]

    @pl.when(core == 1)
    def _():
        pl.semaphore_wait(entered.at[3], 1)
        start(own_sends[2])

    @pl.when(xpos == 0)
    def _():
        pl.semaphore_wait(entered.at[0], 1)
        start(own_sends[0])

    @pl.when(ypos == 0)
    def _():
        pl.semaphore_wait(entered.at[1], 1)
        start(own_sends[1])

    @pl.when(has_up)
    def _():
        pl.semaphore_wait(entered.at[2], 1)
        start(own_z(ALONG_UP))

    row_at = lax.broadcasted_iota(jnp.int32, (width, width), 0)
    col_at = lax.broadcasted_iota(jnp.int32, (width, width), 1)

    own_w.wait()

    @pl.loop(0, sectors)
    def _(s):
        live = (row_at < lsize[s]) & (col_at < rsize[right_of[s]])
        high, low_part = split(jnp.where(live, wbuf[inverse[s]], 0.0))
        rows = pl.ds(pl.multiple_of(s * width, width), width)
        mcat[rows, :width] = high
        mcat[rows, width:] = low_part
        acc[s] = jnp.zeros((width, width), jnp.float32)

    own_r.wait()
    for copy in own_l:
        copy.wait()
    batch = sectors // 2

    def halfway(t, part):
        high, low_part = split(rbuf[t].reshape(rights * width, width))
        doubled = jnp.concatenate([high, high], axis=1)
        contract_last = (((1,), (1,)), ((), ()))
        left = mcat[part * batch * width : (part + 1) * batch * width, :]
        both = lax.dot_general(left, doubled, contract_last, preferred_element_type=jnp.float32)
        both += lax.dot_general(
            left[:, :width], low_part, contract_last, preferred_element_type=jnp.float32
        )
        for j in range(batch):
            s = part * batch + j
            mine = both[j * width : (j + 1) * width]
            which = jnp.full((width, width), right_of[s], jnp.int32)
            pick = mine[:, :width]
            for b in range(1, rights):
                pick = jnp.where(which == b, mine[:, b * width : (b + 1) * width], pick)
            h_high, h_low = split(pick)
            hcat[t, s, :, :width] = h_high
            hcat[t, s, :, width:] = h_low

    def apply_left(s, t):
        high, low_part = split(lbuf[s, t])
        wide = jnp.dot(
            jnp.concatenate([high, low_part], axis=0), hcat[t, s], preferred_element_type=jnp.float32
        )
        acc[s] += wide[:width, :width] + (wide[:width, width:] + wide[width:, :width])

    def run(program, here):
        count = [2, 2, 3 * (here < terms - 1), 3 * (here > 0), 2, 0, 0]

        def send(copy, link):
            copy.start()
            count[link] += 1

        for action in program:
            kind, operand = divmod(action, 100)
            link = {ALONG_X: 0, ALONG_Y: 1, ALONG_UP: 2, ALONG_DOWN: 3}.get(kind)
            if kind == RIGHTS:
                part, t = divmod(operand, 10)
                if t != here and part == 0:
                    await_r(1 - core, t)
                halfway(t, part)
                continue
            if operand >= 40:
                t = operand - 40
                if kind == LAND:
                    await_r(core, t)
                elif kind == SIBLING:
                    send(rpiece(core, t, 4, z, sib), 4)
                else:
                    send(right_z(kind, t), link)
                continue
            place, t = divmod(operand, 4)
            place, i = divmod(place, 2)
            if kind == LAND:
                await_l(place, i, t)
            elif kind == SIBLING:
                send(to_sib(place, i, t), 4 + (place + 1) // 2)
            elif kind == ALONG_X:
                send(to_x(place, i, t), link)
            elif kind == ALONG_Y:
                send(to_y(place, i, t), link)
            elif kind in sides:
                send(to_z(kind, place, i, t), link)
            elif kind == LEFT:
                apply_left(2 * groups[place] + i, t)
            elif kind == SIBLING_LEFT:
                apply_left(2 * flip(groups[place]) + i, t)
            else:
                await_pair(place, t)
        for link, copies in enumerate(count):
            if copies > 0:
                drain(link, copies)

    for here in range(terms):
        @pl.when(z == here)
        def _(here=here):
            run(PROGRAMS[here], here)

    for p in range(sectors):
        s = lsec[p]
        live = (row_at < lsize[s]) & (col_at < rsize[rsec[p]])
        out_ref[p] = jnp.where(live, acc[s], 0.0)


def local_shards(wavefunction, left_sector, right_sector, left_size, right_size, left_ops, right_ops):
    terms = lax.axis_size("ops")
    sectors, width = left_size.shape[0], wavefunction.shape[1]
    rights = right_size.shape[0]
    dma = pltpu.SemaphoreType.DMA
    operands = (
        wavefunction, left_ops, right_ops, left_sector, right_sector, left_size, right_size,
    )
    return pl.pallas_call(
        gather_contract,
        out_shape=pltpu.VMEM(wavefunction.shape, jnp.float32),
        in_specs=[pl.BlockSpec(memory_space=pltpu.HBM)] * 7,
        out_specs=pl.BlockSpec(memory_space=pltpu.VMEM),
        scratch_shapes=[
            pltpu.VMEM(wavefunction.shape, jnp.float32),
            pltpu.VMEM((sectors, terms, width, width), jnp.float32),
            pltpu.VMEM((terms, rights, width, width), jnp.float32),
            pltpu.VMEM((sectors * width, 2 * width), jnp.bfloat16),
            pltpu.VMEM((terms, sectors, width, 2 * width), jnp.bfloat16),
            pltpu.VMEM((sectors, width, width), jnp.float32),
            pltpu.SMEM(left_sector.shape, jnp.int32),
            pltpu.SMEM(right_sector.shape, jnp.int32),
            pltpu.SMEM(left_size.shape, jnp.int32),
            pltpu.SMEM(right_size.shape, jnp.int32),
            pltpu.SMEM((sectors,), jnp.int32),
            pltpu.SMEM((sectors,), jnp.int32),
            dma((6,)),
            dma((4, 2, terms)),
            dma((4, terms)),
            dma((terms, 2)),
            dma((7,)),
            pltpu.SemaphoreType.REGULAR((4,)),
        ],
        compiler_params=pltpu.CompilerParams(collective_id=0, has_side_effects=True, vmem_limit_bytes=40*2**20),
    )(*[pltpu.with_memory_space_constraint(array, pltpu.HBM) for array in operands])


def cube_shards(*arrays):
    wavefunction, left_size, left_ops = arrays[0], arrays[3], arrays[5]
    sectors, width = left_size.shape[0], wavefunction.shape[1]
    terms = lax.axis_size("ops")
    every_sector = wavefunction.shape[0] == sectors
    cube = lax.axis_size("sec") == 2**3 and terms == 2**2 and left_ops.shape[:2] == (2, 1)
    small = sectors * terms * width * width * 4 <= 2**23
    if every_sector and cube and small:
        return local_shards(*arrays)
    return shards(*arrays)


def solution(mesh):
    placed = (
        P(("ops", "sec"), None, None),
        P(("ops", "sec")),
        P(("ops", "sec")),
        P(),
        P(),
        P("sec", "ops", None, None),
        P(None, "ops", None, None),
    )
    return jax.shard_map(
        cube_shards, mesh=mesh, in_specs=placed, out_specs=P(("ops", "sec"), None, None), check_vma=False
    )
```

```python
import jax
import jax.numpy as jnp
from jax import lax
from jax.experimental import pallas as pl
from jax.experimental.pallas import tpu as pltpu
from jax.sharding import PartitionSpec as P

MESH = pl.DeviceIdType.MESH


def contract(running, packed, left_ids, right_ids, live_count, left_blocks, right_blocks):
    turn_count = (live_count + 1) // 2

    def advance(turn_index, current):
        first = 2 * turn_index
        block = lax.dynamic_slice_in_dim(packed, first, 2, 0)
        left_sel = lax.dynamic_slice_in_dim(left_ids, first, 2, 0)
        right_sel = lax.dynamic_slice_in_dim(right_ids, first, 2, 0)
        left_pick = left_blocks[left_sel]
        right_pick = right_blocks[right_sel]
        halfway = jnp.einsum("sij,stlj->stil", block, right_pick, precision=lax.Precision.HIGHEST)
        update = jnp.einsum("stmi,stil->sml", left_pick, halfway, precision=lax.Precision.HIGHEST)
        before = lax.dynamic_slice_in_dim(current, first, 2, 0)
        return lax.dynamic_update_slice_in_dim(current, before + update, first, 0)

    return lax.fori_loop(0, turn_count, advance, running)


def gather_whole(left_ops, right_ops):
    return (
        lax.all_gather(left_ops, "ops", axis=1, tiled=True),
        lax.all_gather(right_ops, "ops", axis=1, tiled=True),
    )


def arrange(incoming, tags, slot_count, width):
    incoming = incoming.reshape(slot_count, width, width)
    tag_ids = tags.reshape(slot_count).astype(jnp.int32)
    live_flag = (tag_ids > 0).astype(jnp.int32)
    order = jnp.argsort(1 - live_flag, stable=True)
    live_count = jnp.sum(live_flag)
    packed = incoming[order]
    right_ids = jnp.maximum(tag_ids[order] - 1, 0)
    return (packed, right_ids, order, live_count)


def shards(wavefunction, left_sector, right_sector, left_size, right_size, left_ops, right_ops):
    peer_count = lax.axis_size("sec")
    sec_local = left_ops.shape[0]
    width = wavefunction.shape[1]
    position = jnp.arange(width)
    left_live = jnp.sum(
        jnp.where(
            left_sector[:, None] == jnp.arange(left_size.shape[0])[None, :], left_size[None, :], 0
        ),
        axis=1,
    )
    right_live = jnp.sum(
        jnp.where(
            right_sector[:, None] == jnp.arange(right_size.shape[0])[None, :],
            right_size[None, :],
            0,
        ),
        axis=1,
    )
    row_live = position[None, :] < left_live[:, None]
    col_live = position[None, :] < right_live[:, None]
    window = (row_live[:, :, None] & col_live[:, None, :]).astype(jnp.float32)
    masked = wavefunction * window
    owner = left_sector // sec_local
    within = left_sector % sec_local
    outgoing = (
        jnp.zeros((peer_count, sec_local, width, width), jnp.float32).at[owner, within].set(masked)
    )
    labels = (
        jnp.zeros((peer_count, sec_local), jnp.float32)
        .at[owner, within]
        .set((right_sector + 1).astype(jnp.float32))
    )
    incoming, tags = (
        lax.all_to_all(outgoing, "sec", split_axis=0, concat_axis=0, tiled=True),
        lax.all_to_all(labels, "sec", split_axis=0, concat_axis=0, tiled=True),
    )
    slot_count = peer_count * sec_local
    packed, right_ids, order, live_count = arrange(incoming, tags, slot_count, width)
    left_ids = order % sec_local
    empty = jnp.zeros_like(packed)
    left_all, right_all = gather_whole(left_ops, right_ops)
    result = contract(empty, packed, left_ids, right_ids, live_count, left_all, right_all)
    restored = jnp.zeros_like(result).at[order].set(result)
    returned = lax.all_to_all(
        restored.reshape(peer_count, sec_local, width, width),
        "sec",
        split_axis=0,
        concat_axis=0,
        tiled=True,
    )
    return returned[owner, within] * window


def split(value):
    high = value.astype(jnp.bfloat16)
    low = (value - high.astype(jnp.float32)).astype(jnp.bfloat16)
    return high, low


LAND, SIBLING, ALONG_X, ALONG_Y, ALONG_UP, ALONG_DOWN, RIGHTS, LEFT, SIBLING_LEFT, LAND_SIBLING, FAR_END = range(11)

PROGRAMS = (
    (
        600, 8, 308, 1, 20, 220, 12, 201, 5, 305, 900, 112, 16, 205, 116, 120,
        41, 141, 301, 610, 716, 916, 105, 101, 28, 428, 24, 108, 2, 124, 202, 302,
        21, 424, 221, 6, 306, 908, 601, 704, 720, 708, 712, 9, 206, 309, 901, 17,
        106, 42, 611, 705, 142, 109, 801, 709, 721, 10, 128, 117, 121, 3, 203, 303,
        102, 602, 612, 800, 29, 7, 107, 207, 307, 902, 13, 22, 113, 924, 18, 820,
        728, 713, 718, 310, 103, 110, 917, 222, 816, 710, 700, 804, 701, 129, 14, 43,
        25, 125, 143, 114, 702, 722, 821, 806, 808, 725, 805, 714, 11, 19, 111, 119,
        122, 925, 118, 603, 613, 828, 829, 15, 903, 115, 23, 910, 909, 27, 123, 127,
        918, 812, 707, 727, 814, 810, 822, 803, 703, 809, 818, 729, 825, 717, 911, 30,
        130, 26, 919, 126, 31, 131, 730, 723, 807, 815, 711, 819, 823, 726, 724, 811,
        719, 802, 817, 706, 824, 715, 731, 813, 926, 927, 831, 827, 830, 826,
    ),
    (
        0, 2, 202, 302, 502, 400, 9, 200, 21, 6, 4, 506, 100, 300, 306, 221,
        404, 40, 309, 204, 140, 42, 542, 601, 17, 18, 440, 142, 3, 503, 901, 104,
        600, 206, 109, 303, 118, 103, 7, 507, 900, 602, 304, 8, 307, 28, 207, 611,
        102, 43, 428, 543, 108, 29, 612, 12, 24, 124, 10, 143, 25, 16, 128, 22,
        107, 310, 203, 122, 13, 125, 424, 113, 106, 121, 610, 702, 924, 718, 706, 728,
        19, 110, 222, 129, 119, 14, 117, 902, 712, 721, 20, 120, 903, 603, 15, 112,
        918, 613, 804, 701, 114, 116, 23, 909, 11, 123, 710, 725, 723, 708, 707, 27,
        115, 925, 127, 703, 813, 704, 916, 824, 26, 30, 130, 31, 126, 806, 131, 805,
        730, 908, 111, 917, 724, 822, 700, 727, 722, 818, 910, 926, 919, 803, 812, 731,
        819, 817, 829, 809, 825, 716, 810, 801, 821, 720, 927, 911, 713, 714, 719, 827,
        814, 815, 820, 711, 816, 811, 826, 830, 715, 807, 800, 828, 808, 831, 802, 709,
        726, 705, 823, 729, 717,
    ),
    (
        3, 203, 503, 1, 303, 401, 602, 201, 612, 7, 207, 5, 22, 507, 301, 405,
        205, 101, 43, 305, 41, 543, 143, 307, 11, 18, 10, 141, 14, 902, 0, 400,
        603, 441, 300, 122, 613, 310, 222, 9, 107, 111, 110, 4, 118, 304, 114, 105,
        200, 17, 15, 404, 19, 806, 21, 706, 309, 40, 440, 103, 117, 140, 27, 910,
        109, 204, 119, 100, 115, 13, 918, 127, 601, 104, 121, 527, 810, 903, 31, 600,
        221, 901, 16, 113, 23, 30, 131, 531, 28, 710, 428, 611, 714, 909, 123, 731,
        707, 814, 610, 24, 424, 116, 128, 8, 26, 911, 130, 12, 900, 807, 803, 727,
        919, 20, 720, 804, 705, 715, 723, 108, 112, 124, 703, 718, 708, 126, 709, 29,
        25, 801, 722, 813, 818, 129, 927, 120, 125, 908, 926, 721, 712, 800, 717, 724,
        729, 716, 826, 831, 815, 924, 917, 702, 916, 925, 830, 700, 719, 819, 809, 811,
        828, 817, 820, 728, 711, 823, 808, 726, 730, 802, 701, 825, 812, 713, 816, 827,
        805, 824, 704, 829, 725, 821, 822,
    ),
    (
        11, 311, 23, 223, 603, 2, 15, 6, 306, 202, 111, 115, 613, 206, 42, 27,
        302, 527, 142, 1, 31, 531, 19, 201, 101, 301, 22, 711, 123, 119, 5, 127,
        222, 911, 305, 106, 602, 18, 205, 131, 10, 0, 1027, 310, 200, 122, 1031, 612,
        9, 14, 102, 927, 811, 903, 41, 309, 109, 118, 831, 17, 141, 919, 727, 710,
        110, 30, 300, 21, 100, 221, 4, 304, 130, 204, 722, 117, 601, 611, 13, 113,
        40, 26, 104, 902, 121, 140, 918, 114, 105, 806, 819, 726, 718, 705, 731, 126,
        815, 807, 701, 715, 702, 802, 714, 707, 730, 823, 600, 723, 8, 910, 909, 25,
        900, 29, 129, 917, 28, 125, 926, 610, 16, 725, 804, 704, 128, 901, 116, 24,
        108, 124, 12, 112, 20, 120, 925, 814, 813, 708, 817, 821, 706, 712, 830, 728,
        822, 810, 729, 721, 713, 829, 809, 724, 825, 826, 924, 916, 908, 816, 818, 827,
        812, 717, 716, 720, 803, 703, 805, 824, 800, 801, 828, 719, 808, 709, 820, 700,
    ),
)


def gather_contract(
    wf_hbm, lops_hbm, rops_hbm, lsec_hbm, rsec_hbm, lsize_hbm, rsize_hbm,
    out_ref,
    wbuf, lbuf, rbuf, mcat, hcat, acc, lsec, rsec, lsize, rsize, inverse, right_of,
    own_sem, recv_own, recv_sib, recv_r, sends, entered,
):
    terms = lax.axis_size("ops")
    sectors, _, width, _ = lbuf.shape
    rights = rbuf.shape[1]
    half = width // 2
    z = lax.axis_index("ops")
    sec = lax.axis_index("sec")
    core = sec % 2
    xpos = (sec // 2) % 2
    ypos = sec // 4
    sib = sec + 1 - 2 * core
    xnb = sec + 2 - 4 * xpos
    ynb = sec + 4 - 8 * ypos
    dnb = xnb + 4 - 8 * ypos
    has_up = z < terms - 1
    has_dn = z > 0

    def flip(group):
        return group + 1 - 2 * core

    barrier = pltpu.get_barrier_semaphore()

    def greet(sem, zz, ss):
        pl.semaphore_signal(sem, inc=1, device_id=(zz, ss), device_id_type=MESH)

    links = (
        (xpos == 0, xpos == 1, z, xnb),
        (ypos == 0, ypos == 1, z, ynb),
        (has_up, has_dn, z, sec),
        (core == 1, core == 0, z, sib),
    )
    for k, (first, second, zz, ss) in enumerate(links):
        @pl.when(first)
        def _(k=k, zz=zz, ss=ss):
            greet(barrier, zz + 1 if k == 2 else zz, ss)

    scalar_in = [
        pltpu.make_async_copy(src, dst, own_sem.at[2 + n])
        for n, (src, dst) in enumerate(
            ((lsec_hbm, lsec), (rsec_hbm, rsec), (lsize_hbm, lsize), (rsize_hbm, rsize))
        )
    ]
    own_l = [
        pltpu.make_async_copy(lops_hbm.at[i, 0], lbuf.at[2 * sec + i, z], recv_own.at[0, i, z])
        for i in range(2)
    ]
    own_r = pltpu.make_async_copy(rops_hbm.at[:, 0], rbuf.at[z], own_sem.at[0])
    own_w = pltpu.make_async_copy(wf_hbm, wbuf, own_sem.at[1])
    for copy in scalar_in:
        copy.start()
    own_w.start()
    own_r.start()
    for copy in own_l:
        copy.start()
    firsts = xpos + ypos + has_dn.astype(jnp.int32) + 1 - core

    @pl.when(firsts > 0)
    def _():
        pl.semaphore_wait(barrier, firsts)

    for k, (first, second, zz, ss) in enumerate(links):
        @pl.when(second)
        def _(k=k, zz=zz, ss=ss):
            greet(entered.at[k], zz - 1 if k == 2 else zz, ss)

    def move(src, dst, ssem, rsem, zz, ss):
        return pltpu.make_async_remote_copy(
            src_ref=src, dst_ref=dst, send_sem=ssem, recv_sem=rsem,
            device_id=(zz, ss), device_id_type=MESH,
        )

    def piece(group, i, t, link, rsem, zz, ss, own=False):
        s = 2 * group + i
        src = lops_hbm.at[i, 0] if own else lbuf.at[s, t]
        return move(src, lbuf.at[s, t], sends.at[link], rsem, zz, ss)

    def rpiece(h, t, link, zz, ss, own=False):
        rows = pl.ds(pl.multiple_of(h * half, half), half)
        src = rops_hbm.at[:, 0, rows] if own else rbuf.at[t, :, rows]
        return move(src, rbuf.at[t, :, rows], sends.at[link], recv_r.at[t, h], zz, ss)

    def await_l(place, i, t):
        group = groups[place]
        piece(group, i, t, 0, recv_own.at[place, i, t], z, xnb).wait_recv()

    def await_pair(place, t):
        first = 2 * flip(groups[place])
        pair = lbuf.at[pl.ds(first, 2), t]
        move(pair, pair, sends.at[0], recv_sib.at[place, t], z, sib).wait_recv()

    def await_r(h, t):
        rpiece(h, t, 0, z, xnb).wait_recv()

    def drain(link, count):
        blocks = wbuf.at[pl.ds(0, count)]
        move(blocks, blocks, sends.at[link], recv_own.at[0, 0, 0], z, xnb).wait_send()

    groups = (sec, xnb, ynb, dnb)
    sides = {ALONG_UP: (2, 1), ALONG_DOWN: (3, -1)}

    def to_z(way, place, i, t, own=False):
        link, step = sides[way]
        return piece(groups[place], i, t, link, recv_own.at[place, i, t], z + step, sec, own)

    def to_far_end(place, i, t):
        return piece(groups[place], i, t, 3, recv_own.at[place, i, t], z + 1 - terms, sec)

    def right_z(way, t, own=False):
        link, step = sides[way]
        return rpiece(core, t, link, z + step, sec, own)

    def to_x(place, i, t, own=False):
        return piece(groups[place], i, t, 0, recv_own.at[place + 1, i, t], z, xnb, own)

    def to_y(place, i, t, own=False):
        return piece(groups[place], i, t, 1, recv_own.at[place + 2, i, t], z, ynb, own)

    def to_sib(place, i, t, own=False):
        link = 4 + (place + 1) // 2
        return piece(groups[place], i, t, link, recv_sib.at[place, t], z, sib, own)

    def own_z(way):
        return [to_z(way, 0, 0, z, True), to_z(way, 0, 1, z, True), right_z(way, z, True)]

    own_sends = (
        [to_x(0, 0, z, True), to_x(0, 1, z, True)],
        [to_y(0, 1, z, True), to_y(0, 0, z, True)],
        [to_sib(0, 0, z, True), to_sib(0, 1, z, True)],
    )

    def start(copies):
        for copy in copies:
            copy.start()

    @pl.when(xpos == 1)
    def _():
        start(own_sends[0])

    @pl.when(ypos == 1)
    def _():
        start(own_sends[1])

    @pl.when(has_dn)
    def _():
        start(own_z(ALONG_DOWN))

    @pl.when(core == 0)
    def _():
        start(own_sends[2])

    for copy in scalar_in:
        copy.wait()
    for s in range(sectors):
        value = jnp.int32(0)
        for p in range(1, sectors):
            value = jnp.where(lsec[p] == s, p, value)
        inverse[s] = value
        right_of[s] = rsec[value]

    @pl.when(core == 1)
    def _():
        pl.semaphore_wait(entered.at[3], 1)
        start(own_sends[2])

    @pl.when(xpos == 0)
    def _():
        pl.semaphore_wait(entered.at[0], 1)
        start(own_sends[0])

    @pl.when(ypos == 0)
    def _():
        pl.semaphore_wait(entered.at[1], 1)
        start(own_sends[1])

    @pl.when(has_up)
    def _():
        pl.semaphore_wait(entered.at[2], 1)
        start(own_z(ALONG_UP))

    row_at = lax.broadcasted_iota(jnp.int32, (width, width), 0)
    col_at = lax.broadcasted_iota(jnp.int32, (width, width), 1)

    own_w.wait()

    @pl.loop(0, sectors)
    def _(s):
        live = (row_at < lsize[s]) & (col_at < rsize[right_of[s]])
        high, low_part = split(jnp.where(live, wbuf[inverse[s]], 0.0))
        rows = pl.ds(pl.multiple_of(s * width, width), width)
        mcat[rows, :width] = high
        mcat[rows, width:] = low_part
        acc[s] = jnp.zeros((width, width), jnp.float32)

    own_r.wait()
    for copy in own_l:
        copy.wait()
    batch = sectors // 2

    def halfway(t, part):
        high, low_part = split(rbuf[t].reshape(rights * width, width))
        doubled = jnp.concatenate([high, high], axis=1)
        contract_last = (((1,), (1,)), ((), ()))
        left = mcat[part * batch * width : (part + 1) * batch * width, :]
        both = lax.dot_general(left, doubled, contract_last, preferred_element_type=jnp.float32)
        both += lax.dot_general(
            left[:, :width], low_part, contract_last, preferred_element_type=jnp.float32
        )
        for j in range(batch):
            s = part * batch + j
            mine = both[j * width : (j + 1) * width]
            which = jnp.full((width, width), right_of[s], jnp.int32)
            pick = mine[:, :width]
            for b in range(1, rights):
                pick = jnp.where(which == b, mine[:, b * width : (b + 1) * width], pick)
            h_high, h_low = split(pick)
            hcat[t, s, :, :width] = h_high
            hcat[t, s, :, width:] = h_low

    def apply_left(s, t):
        high, low_part = split(lbuf[s, t])
        wide = jnp.dot(
            jnp.concatenate([high, low_part], axis=0), hcat[t, s], preferred_element_type=jnp.float32
        )
        acc[s] += wide[:width, :width] + (wide[:width, width:] + wide[width:, :width])

    def run(program, here):
        count = [2, 2, 3 * (here < terms - 1), 3 * (here > 0), 2, 0, 0]

        def send(copy, link):
            copy.start()
            count[link] += 1

        for action in program:
            kind, operand = divmod(action, 100)
            link = {ALONG_X: 0, ALONG_Y: 1, ALONG_UP: 2, ALONG_DOWN: 3}.get(kind)
            if kind == RIGHTS:
                part, t = divmod(operand, 10)
                if t != here and part == 0:
                    await_r(1 - core, t)
                halfway(t, part)
                continue
            if operand >= 40:
                t = operand - 40
                if kind == LAND:
                    await_r(core, t)
                elif kind == SIBLING:
                    send(rpiece(core, t, 4, z, sib), 4)
                else:
                    send(right_z(kind, t), link)
                continue
            place, t = divmod(operand, 4)
            place, i = divmod(place, 2)
            if kind == LAND:
                await_l(place, i, t)
            elif kind == SIBLING:
                send(to_sib(place, i, t), 4 + (place + 1) // 2)
            elif kind == ALONG_X:
                send(to_x(place, i, t), link)
            elif kind == ALONG_Y:
                send(to_y(place, i, t), link)
            elif kind in sides:
                send(to_z(kind, place, i, t), link)
            elif kind == FAR_END:
                send(to_far_end(place, i, t), 3)
            elif kind == LEFT:
                apply_left(2 * groups[place] + i, t)
            elif kind == SIBLING_LEFT:
                apply_left(2 * flip(groups[place]) + i, t)
            else:
                await_pair(place, t)
        for link, copies in enumerate(count):
            if copies > 0:
                drain(link, copies)

    for here in range(terms):
        @pl.when(z == here)
        def _(here=here):
            run(PROGRAMS[here], here)

    for p in range(sectors):
        s = lsec[p]
        live = (row_at < lsize[s]) & (col_at < rsize[rsec[p]])
        out_ref[p] = jnp.where(live, acc[s], 0.0)


def local_shards(wavefunction, left_sector, right_sector, left_size, right_size, left_ops, right_ops):
    terms = lax.axis_size("ops")
    sectors, width = left_size.shape[0], wavefunction.shape[1]
    rights = right_size.shape[0]
    dma = pltpu.SemaphoreType.DMA
    operands = (
        wavefunction, left_ops, right_ops, left_sector, right_sector, left_size, right_size,
    )
    return pl.pallas_call(
        gather_contract,
        out_shape=pltpu.VMEM(wavefunction.shape, jnp.float32),
        in_specs=[pl.BlockSpec(memory_space=pltpu.HBM)] * 7,
        out_specs=pl.BlockSpec(memory_space=pltpu.VMEM),
        scratch_shapes=[
            pltpu.VMEM(wavefunction.shape, jnp.float32),
            pltpu.VMEM((sectors, terms, width, width), jnp.float32),
            pltpu.VMEM((terms, rights, width, width), jnp.float32),
            pltpu.VMEM((sectors * width, 2 * width), jnp.bfloat16),
            pltpu.VMEM((terms, sectors, width, 2 * width), jnp.bfloat16),
            pltpu.VMEM((sectors, width, width), jnp.float32),
            pltpu.SMEM(left_sector.shape, jnp.int32),
            pltpu.SMEM(right_sector.shape, jnp.int32),
            pltpu.SMEM(left_size.shape, jnp.int32),
            pltpu.SMEM(right_size.shape, jnp.int32),
            pltpu.SMEM((sectors,), jnp.int32),
            pltpu.SMEM((sectors,), jnp.int32),
            dma((6,)),
            dma((4, 2, terms)),
            dma((4, terms)),
            dma((terms, 2)),
            dma((7,)),
            pltpu.SemaphoreType.REGULAR((4,)),
        ],
        compiler_params=pltpu.CompilerParams(collective_id=0, has_side_effects=True, vmem_limit_bytes=40*2**20),
    )(*[pltpu.with_memory_space_constraint(array, pltpu.HBM) for array in operands])


def cube_shards(*arrays):
    wavefunction, left_size, left_ops = arrays[0], arrays[3], arrays[5]
    sectors, width = left_size.shape[0], wavefunction.shape[1]
    terms = lax.axis_size("ops")
    every_sector = wavefunction.shape[0] == sectors
    cube = lax.axis_size("sec") == 2**3 and terms == 2**2 and left_ops.shape[:2] == (2, 1)
    small = sectors * terms * width * width * 4 <= 2**23
    if every_sector and cube and small:
        return local_shards(*arrays)
    return shards(*arrays)


def solution(mesh):
    placed = (
        P(("ops", "sec"), None, None),
        P(("ops", "sec")),
        P(("ops", "sec")),
        P(),
        P(),
        P("sec", "ops", None, None),
        P(None, "ops", None, None),
    )
    return jax.shard_map(
        cube_shards, mesh=mesh, in_specs=placed, out_specs=P(("ops", "sec"), None, None), check_vma=False
    )
```

```python
import jax
import jax.numpy as jnp
from jax import lax
from jax.experimental import pallas as pl
from jax.experimental.pallas import tpu as pltpu
from jax.sharding import PartitionSpec as P

MESH = pl.DeviceIdType.MESH


def contract(running, packed, left_ids, right_ids, live_count, left_blocks, right_blocks):
    turn_count = (live_count + 1) // 2

    def advance(turn_index, current):
        first = 2 * turn_index
        block = lax.dynamic_slice_in_dim(packed, first, 2, 0)
        left_sel = lax.dynamic_slice_in_dim(left_ids, first, 2, 0)
        right_sel = lax.dynamic_slice_in_dim(right_ids, first, 2, 0)
        left_pick = left_blocks[left_sel]
        right_pick = right_blocks[right_sel]
        halfway = jnp.einsum("sij,stlj->stil", block, right_pick, precision=lax.Precision.HIGHEST)
        update = jnp.einsum("stmi,stil->sml", left_pick, halfway, precision=lax.Precision.HIGHEST)
        before = lax.dynamic_slice_in_dim(current, first, 2, 0)
        return lax.dynamic_update_slice_in_dim(current, before + update, first, 0)

    return lax.fori_loop(0, turn_count, advance, running)


def gather_whole(left_ops, right_ops):
    return (
        lax.all_gather(left_ops, "ops", axis=1, tiled=True),
        lax.all_gather(right_ops, "ops", axis=1, tiled=True),
    )


def arrange(incoming, tags, slot_count, width):
    incoming = incoming.reshape(slot_count, width, width)
    tag_ids = tags.reshape(slot_count).astype(jnp.int32)
    live_flag = (tag_ids > 0).astype(jnp.int32)
    order = jnp.argsort(1 - live_flag, stable=True)
    live_count = jnp.sum(live_flag)
    packed = incoming[order]
    right_ids = jnp.maximum(tag_ids[order] - 1, 0)
    return (packed, right_ids, order, live_count)


def shards(wavefunction, left_sector, right_sector, left_size, right_size, left_ops, right_ops):
    peer_count = lax.axis_size("sec")
    sec_local = left_ops.shape[0]
    width = wavefunction.shape[1]
    position = jnp.arange(width)
    left_live = jnp.sum(
        jnp.where(
            left_sector[:, None] == jnp.arange(left_size.shape[0])[None, :], left_size[None, :], 0
        ),
        axis=1,
    )
    right_live = jnp.sum(
        jnp.where(
            right_sector[:, None] == jnp.arange(right_size.shape[0])[None, :],
            right_size[None, :],
            0,
        ),
        axis=1,
    )
    row_live = position[None, :] < left_live[:, None]
    col_live = position[None, :] < right_live[:, None]
    window = (row_live[:, :, None] & col_live[:, None, :]).astype(jnp.float32)
    masked = wavefunction * window
    owner = left_sector // sec_local
    within = left_sector % sec_local
    outgoing = (
        jnp.zeros((peer_count, sec_local, width, width), jnp.float32).at[owner, within].set(masked)
    )
    labels = (
        jnp.zeros((peer_count, sec_local), jnp.float32)
        .at[owner, within]
        .set((right_sector + 1).astype(jnp.float32))
    )
    incoming, tags = (
        lax.all_to_all(outgoing, "sec", split_axis=0, concat_axis=0, tiled=True),
        lax.all_to_all(labels, "sec", split_axis=0, concat_axis=0, tiled=True),
    )
    slot_count = peer_count * sec_local
    packed, right_ids, order, live_count = arrange(incoming, tags, slot_count, width)
    left_ids = order % sec_local
    empty = jnp.zeros_like(packed)
    left_all, right_all = gather_whole(left_ops, right_ops)
    result = contract(empty, packed, left_ids, right_ids, live_count, left_all, right_all)
    restored = jnp.zeros_like(result).at[order].set(result)
    returned = lax.all_to_all(
        restored.reshape(peer_count, sec_local, width, width),
        "sec",
        split_axis=0,
        concat_axis=0,
        tiled=True,
    )
    return returned[owner, within] * window


def split(value):
    high = value.astype(jnp.bfloat16)
    low = (value - high.astype(jnp.float32)).astype(jnp.bfloat16)
    return high, low


LAND, SIBLING, ALONG_X, ALONG_Y, ALONG_UP, ALONG_DOWN, RIGHTS, LEFT, SIBLING_LEFT, LAND_SIBLING, FAR_END = range(11)

PROGRAMS = (
    (
        600, 8, 308, 1, 20, 220, 12, 201, 5, 305, 900, 112, 16, 205, 116, 120,
        41, 141, 301, 610, 716, 916, 105, 101, 28, 428, 24, 108, 2, 124, 202, 302,
        21, 424, 221, 6, 306, 908, 601, 704, 720, 708, 712, 9, 206, 309, 901, 17,
        106, 42, 611, 705, 142, 109, 801, 709, 721, 10, 128, 117, 121, 3, 203, 303,
        102, 602, 612, 800, 29, 7, 107, 207, 307, 902, 13, 22, 113, 924, 18, 820,
        728, 713, 718, 310, 103, 110, 917, 222, 816, 710, 700, 804, 701, 129, 14, 43,
        25, 125, 143, 114, 702, 722, 821, 806, 808, 725, 805, 714, 11, 19, 111, 119,
        122, 925, 118, 603, 613, 828, 829, 15, 903, 115, 23, 910, 909, 27, 123, 127,
        918, 812, 707, 727, 814, 810, 822, 803, 703, 809, 818, 729, 825, 717, 911, 30,
        130, 26, 919, 126, 31, 131, 730, 723, 807, 815, 711, 819, 823, 726, 724, 811,
        719, 802, 817, 706, 824, 715, 731, 813, 926, 927, 831, 827, 830, 826,
    ),
    (
        0, 2, 202, 302, 502, 400, 9, 200, 21, 6, 4, 506, 100, 300, 306, 221,
        404, 40, 309, 204, 140, 42, 542, 601, 17, 18, 440, 142, 3, 503, 901, 104,
        600, 206, 109, 303, 118, 103, 7, 507, 900, 602, 304, 8, 307, 28, 207, 611,
        102, 43, 428, 543, 108, 29, 612, 12, 24, 124, 10, 143, 25, 16, 128, 22,
        107, 310, 203, 122, 13, 125, 424, 113, 106, 121, 610, 702, 924, 718, 706, 728,
        19, 110, 222, 129, 119, 14, 117, 902, 712, 721, 20, 120, 903, 603, 15, 112,
        918, 613, 804, 701, 114, 116, 23, 909, 11, 123, 710, 725, 723, 708, 707, 27,
        115, 925, 127, 703, 813, 704, 916, 824, 26, 30, 130, 31, 126, 806, 131, 805,
        730, 908, 111, 917, 724, 822, 700, 727, 722, 818, 910, 926, 919, 803, 812, 731,
        819, 817, 829, 809, 825, 716, 810, 801, 821, 720, 927, 911, 713, 714, 719, 827,
        814, 815, 820, 711, 816, 811, 826, 830, 715, 807, 800, 828, 808, 831, 802, 709,
        726, 705, 823, 729, 717,
    ),
    (
        3, 203, 503, 1, 303, 401, 602, 201, 612, 7, 207, 5, 22, 507, 301, 405,
        205, 101, 43, 305, 41, 543, 143, 307, 11, 18, 10, 141, 14, 902, 0, 400,
        603, 441, 300, 122, 613, 310, 222, 9, 107, 111, 110, 4, 118, 304, 114, 105,
        200, 17, 15, 404, 19, 806, 21, 706, 309, 40, 440, 103, 117, 140, 27, 910,
        109, 204, 119, 100, 115, 13, 918, 127, 601, 104, 121, 527, 810, 903, 31, 600,
        221, 901, 16, 113, 23, 30, 131, 531, 28, 710, 428, 611, 714, 909, 123, 731,
        707, 814, 610, 24, 424, 116, 128, 8, 26, 911, 130, 12, 900, 807, 803, 727,
        919, 20, 720, 804, 705, 715, 723, 108, 112, 124, 703, 718, 708, 126, 709, 29,
        25, 801, 722, 813, 818, 129, 927, 120, 125, 908, 926, 721, 712, 800, 717, 724,
        729, 716, 826, 831, 815, 924, 917, 702, 916, 925, 830, 700, 719, 819, 809, 811,
        828, 817, 820, 728, 711, 823, 808, 726, 730, 802, 701, 825, 812, 713, 816, 827,
        805, 824, 704, 829, 725, 821, 822,
    ),
    (
        11, 311, 23, 223, 603, 2, 15, 6, 306, 202, 111, 115, 613, 206, 42, 27,
        302, 527, 142, 1, 31, 531, 19, 201, 101, 301, 22, 711, 123, 119, 5, 127,
        222, 911, 305, 106, 602, 18, 205, 131, 10, 0, 1027, 1031, 310, 200, 122, 612,
        9, 14, 102, 927, 811, 903, 41, 309, 109, 118, 831, 17, 141, 919, 727, 710,
        110, 30, 300, 21, 100, 221, 4, 304, 130, 204, 722, 117, 601, 611, 13, 113,
        40, 26, 104, 902, 121, 140, 918, 114, 105, 806, 819, 726, 718, 705, 731, 126,
        815, 807, 701, 715, 702, 802, 714, 707, 730, 823, 600, 723, 8, 910, 909, 25,
        900, 29, 129, 917, 28, 125, 926, 610, 16, 725, 804, 704, 128, 901, 116, 24,
        108, 124, 12, 112, 20, 120, 925, 814, 813, 708, 817, 821, 706, 712, 830, 728,
        822, 810, 729, 721, 713, 829, 809, 724, 825, 826, 924, 916, 908, 816, 818, 827,
        812, 717, 716, 720, 803, 703, 805, 824, 800, 801, 828, 719, 808, 709, 820, 700,
    ),
)


def gather_contract(
    wf_hbm, lops_hbm, rops_hbm, lsec_hbm, rsec_hbm, lsize_hbm, rsize_hbm,
    out_ref,
    wbuf, lbuf, rbuf, mcat, hcat, acc, lsec, rsec, lsize, rsize, inverse, right_of,
    own_sem, recv_own, recv_sib, recv_r, sends, entered,
):
    terms = lax.axis_size("ops")
    sectors, _, width, _ = lbuf.shape
    rights = rbuf.shape[1]
    half = width // 2
    z = lax.axis_index("ops")
    sec = lax.axis_index("sec")
    core = sec % 2
    xpos = (sec // 2) % 2
    ypos = sec // 4
    sib = sec + 1 - 2 * core
    xnb = sec + 2 - 4 * xpos
    ynb = sec + 4 - 8 * ypos
    dnb = xnb + 4 - 8 * ypos
    has_up = z < terms - 1
    has_dn = z > 0

    def flip(group):
        return group + 1 - 2 * core

    barrier = pltpu.get_barrier_semaphore()

    def greet(sem, zz, ss):
        pl.semaphore_signal(sem, inc=1, device_id=(zz, ss), device_id_type=MESH)

    links = (
        (xpos == 0, xpos == 1, z, xnb),
        (ypos == 0, ypos == 1, z, ynb),
        (has_up, has_dn, z, sec),
        (core == 1, core == 0, z, sib),
    )
    for k, (first, second, zz, ss) in enumerate(links):
        @pl.when(first)
        def _(k=k, zz=zz, ss=ss):
            greet(barrier, zz + 1 if k == 2 else zz, ss)

    scalar_in = [
        pltpu.make_async_copy(src, dst, own_sem.at[2 + n])
        for n, (src, dst) in enumerate(
            ((lsec_hbm, lsec), (rsec_hbm, rsec), (lsize_hbm, lsize), (rsize_hbm, rsize))
        )
    ]
    own_l = [
        pltpu.make_async_copy(lops_hbm.at[i, 0], lbuf.at[2 * sec + i, z], recv_own.at[0, i, z])
        for i in range(2)
    ]
    own_r = pltpu.make_async_copy(rops_hbm.at[:, 0], rbuf.at[z], own_sem.at[0])
    own_w = pltpu.make_async_copy(wf_hbm, wbuf, own_sem.at[1])
    for copy in scalar_in:
        copy.start()
    own_w.start()
    own_r.start()
    for copy in own_l:
        copy.start()
    firsts = xpos + ypos + has_dn.astype(jnp.int32) + 1 - core

    @pl.when(firsts > 0)
    def _():
        pl.semaphore_wait(barrier, firsts)

    for k, (first, second, zz, ss) in enumerate(links):
        @pl.when(second)
        def _(k=k, zz=zz, ss=ss):
            greet(entered.at[k], zz - 1 if k == 2 else zz, ss)

    def move(src, dst, ssem, rsem, zz, ss):
        return pltpu.make_async_remote_copy(
            src_ref=src, dst_ref=dst, send_sem=ssem, recv_sem=rsem,
            device_id=(zz, ss), device_id_type=MESH,
        )

    def piece(group, i, t, link, rsem, zz, ss, own=False):
        s = 2 * group + i
        src = lops_hbm.at[i, 0] if own else lbuf.at[s, t]
        return move(src, lbuf.at[s, t], sends.at[link], rsem, zz, ss)

    def rpiece(h, t, link, zz, ss, own=False):
        rows = pl.ds(pl.multiple_of(h * half, half), half)
        src = rops_hbm.at[:, 0, rows] if own else rbuf.at[t, :, rows]
        return move(src, rbuf.at[t, :, rows], sends.at[link], recv_r.at[t, h], zz, ss)

    def await_l(place, i, t):
        group = groups[place]
        piece(group, i, t, 0, recv_own.at[place, i, t], z, xnb).wait_recv()

    def await_pair(place, t):
        first = 2 * flip(groups[place])
        pair = lbuf.at[pl.ds(first, 2), t]
        move(pair, pair, sends.at[0], recv_sib.at[place, t], z, sib).wait_recv()

    def await_r(h, t):
        rpiece(h, t, 0, z, xnb).wait_recv()

    def drain(link, count):
        blocks = wbuf.at[pl.ds(0, count)]
        move(blocks, blocks, sends.at[link], recv_own.at[0, 0, 0], z, xnb).wait_send()

    groups = (sec, xnb, ynb, dnb)
    sides = {ALONG_UP: (2, 1), ALONG_DOWN: (3, -1)}

    def to_z(way, place, i, t, own=False):
        link, step = sides[way]
        return piece(groups[place], i, t, link, recv_own.at[place, i, t], z + step, sec, own)

    def to_far_end(place, i, t):
        return piece(groups[place], i, t, 3, recv_own.at[place, i, t], z + 1 - terms, sec)

    def right_z(way, t, own=False):
        link, step = sides[way]
        return rpiece(core, t, link, z + step, sec, own)

    def to_x(place, i, t, own=False):
        return piece(groups[place], i, t, 0, recv_own.at[place + 1, i, t], z, xnb, own)

    def to_y(place, i, t, own=False):
        return piece(groups[place], i, t, 1, recv_own.at[place + 2, i, t], z, ynb, own)

    def to_sib(place, i, t, own=False):
        link = 4 + (place + 1) // 2
        return piece(groups[place], i, t, link, recv_sib.at[place, t], z, sib, own)

    def own_z(way, own):
        return [to_z(way, 0, 0, z, own), to_z(way, 0, 1, z, own), right_z(way, z, own)]

    def own_sends(own):
        return (
            [to_x(0, 0, z, own), to_x(0, 1, z, own)],
            [to_y(0, 1, z, own), to_y(0, 0, z, own)],
            [to_sib(0, 0, z, own), to_sib(0, 1, z, own)],
        )

    def start(copies):
        for copy in copies:
            copy.start()

    @pl.when(xpos == 1)
    def _():
        start(own_sends(True)[0])

    @pl.when(ypos == 1)
    def _():
        start(own_sends(True)[1])

    @pl.when(has_dn)
    def _():
        start(own_z(ALONG_DOWN, True))

    @pl.when(core == 0)
    def _():
        start(own_sends(True)[2])

    for copy in scalar_in:
        copy.wait()
    for s in range(sectors):
        value = jnp.int32(0)
        for p in range(1, sectors):
            value = jnp.where(lsec[p] == s, p, value)
        inverse[s] = value
        right_of[s] = rsec[value]

    own_r.wait()
    for copy in own_l:
        copy.wait()

    @pl.when(core == 1)
    def _():
        pl.semaphore_wait(entered.at[3], 1)
        start(own_sends(False)[2])

    @pl.when(xpos == 0)
    def _():
        pl.semaphore_wait(entered.at[0], 1)
        start(own_sends(False)[0])

    @pl.when(ypos == 0)
    def _():
        pl.semaphore_wait(entered.at[1], 1)
        start(own_sends(False)[1])

    @pl.when(has_up)
    def _():
        pl.semaphore_wait(entered.at[2], 1)
        start(own_z(ALONG_UP, False))

    row_at = lax.broadcasted_iota(jnp.int32, (width, width), 0)
    col_at = lax.broadcasted_iota(jnp.int32, (width, width), 1)

    own_w.wait()

    @pl.loop(0, sectors)
    def _(s):
        live = (row_at < lsize[s]) & (col_at < rsize[right_of[s]])
        high, low_part = split(jnp.where(live, wbuf[inverse[s]], 0.0))
        rows = pl.ds(pl.multiple_of(s * width, width), width)
        mcat[rows, :width] = high
        mcat[rows, width:] = low_part
        acc[s] = jnp.zeros((width, width), jnp.float32)

    batch = sectors // 2

    def halfway(t, part):
        high, low_part = split(rbuf[t].reshape(rights * width, width))
        doubled = jnp.concatenate([high, high], axis=1)
        contract_last = (((1,), (1,)), ((), ()))
        left = mcat[part * batch * width : (part + 1) * batch * width, :]
        both = lax.dot_general(left, doubled, contract_last, preferred_element_type=jnp.float32)
        both += lax.dot_general(
            left[:, :width], low_part, contract_last, preferred_element_type=jnp.float32
        )
        for j in range(batch):
            s = part * batch + j
            mine = both[j * width : (j + 1) * width]
            which = jnp.full((width, width), right_of[s], jnp.int32)
            pick = mine[:, :width]
            for b in range(1, rights):
                pick = jnp.where(which == b, mine[:, b * width : (b + 1) * width], pick)
            h_high, h_low = split(pick)
            hcat[t, s, :, :width] = h_high
            hcat[t, s, :, width:] = h_low

    def apply_left(s, t):
        high, low_part = split(lbuf[s, t])
        wide = jnp.dot(
            jnp.concatenate([high, low_part], axis=0), hcat[t, s], preferred_element_type=jnp.float32
        )
        acc[s] += wide[:width, :width] + (wide[:width, width:] + wide[width:, :width])

    def run(program, here):
        count = [2, 2, 3 * (here < terms - 1), 3 * (here > 0), 2, 0, 0]

        def send(copy, link):
            copy.start()
            count[link] += 1

        for action in program:
            kind, operand = divmod(action, 100)
            link = {ALONG_X: 0, ALONG_Y: 1, ALONG_UP: 2, ALONG_DOWN: 3}.get(kind)
            if kind == RIGHTS:
                part, t = divmod(operand, 10)
                if t != here and part == 0:
                    await_r(1 - core, t)
                halfway(t, part)
                continue
            if operand >= 40:
                t = operand - 40
                if kind == LAND:
                    await_r(core, t)
                elif kind == SIBLING:
                    send(rpiece(core, t, 4, z, sib), 4)
                else:
                    send(right_z(kind, t), link)
                continue
            place, t = divmod(operand, 4)
            place, i = divmod(place, 2)
            if kind == LAND:
                await_l(place, i, t)
            elif kind == SIBLING:
                send(to_sib(place, i, t), 4 + (place + 1) // 2)
            elif kind == ALONG_X:
                send(to_x(place, i, t), link)
            elif kind == ALONG_Y:
                send(to_y(place, i, t), link)
            elif kind in sides:
                send(to_z(kind, place, i, t), link)
            elif kind == FAR_END:
                send(to_far_end(place, i, t), 3)
            elif kind == LEFT:
                apply_left(2 * groups[place] + i, t)
            elif kind == SIBLING_LEFT:
                apply_left(2 * flip(groups[place]) + i, t)
            else:
                await_pair(place, t)
        for link, copies in enumerate(count):
            if copies > 0:
                drain(link, copies)

    for here in range(terms):
        @pl.when(z == here)
        def _(here=here):
            run(PROGRAMS[here], here)

    for p in range(sectors):
        s = lsec[p]
        live = (row_at < lsize[s]) & (col_at < rsize[rsec[p]])
        out_ref[p] = jnp.where(live, acc[s], 0.0)


def local_shards(wavefunction, left_sector, right_sector, left_size, right_size, left_ops, right_ops):
    terms = lax.axis_size("ops")
    sectors, width = left_size.shape[0], wavefunction.shape[1]
    rights = right_size.shape[0]
    dma = pltpu.SemaphoreType.DMA
    operands = (
        wavefunction, left_ops, right_ops, left_sector, right_sector, left_size, right_size,
    )
    return pl.pallas_call(
        gather_contract,
        out_shape=pltpu.VMEM(wavefunction.shape, jnp.float32),
        in_specs=[pl.BlockSpec(memory_space=pltpu.HBM)] * 7,
        out_specs=pl.BlockSpec(memory_space=pltpu.VMEM),
        scratch_shapes=[
            pltpu.VMEM(wavefunction.shape, jnp.float32),
            pltpu.VMEM((sectors, terms, width, width), jnp.float32),
            pltpu.VMEM((terms, rights, width, width), jnp.float32),
            pltpu.VMEM((sectors * width, 2 * width), jnp.bfloat16),
            pltpu.VMEM((terms, sectors, width, 2 * width), jnp.bfloat16),
            pltpu.VMEM((sectors, width, width), jnp.float32),
            pltpu.SMEM(left_sector.shape, jnp.int32),
            pltpu.SMEM(right_sector.shape, jnp.int32),
            pltpu.SMEM(left_size.shape, jnp.int32),
            pltpu.SMEM(right_size.shape, jnp.int32),
            pltpu.SMEM((sectors,), jnp.int32),
            pltpu.SMEM((sectors,), jnp.int32),
            dma((6,)),
            dma((4, 2, terms)),
            dma((4, terms)),
            dma((terms, 2)),
            dma((7,)),
            pltpu.SemaphoreType.REGULAR((4,)),
        ],
        compiler_params=pltpu.CompilerParams(collective_id=0, has_side_effects=True, vmem_limit_bytes=40*2**20),
    )(*[pltpu.with_memory_space_constraint(array, pltpu.HBM) for array in operands])


def cube_shards(*arrays):
    wavefunction, left_size, left_ops = arrays[0], arrays[3], arrays[5]
    sectors, width = left_size.shape[0], wavefunction.shape[1]
    terms = lax.axis_size("ops")
    every_sector = wavefunction.shape[0] == sectors
    cube = lax.axis_size("sec") == 2**3 and terms == 2**2 and left_ops.shape[:2] == (2, 1)
    cube = cube and arrays[4].shape[0] == 2
    small = sectors * terms * width * width * 4 <= 2**23
    if every_sector and cube and small:
        return local_shards(*arrays)
    return shards(*arrays)


def solution(mesh):
    placed = (
        P(("ops", "sec"), None, None),
        P(("ops", "sec")),
        P(("ops", "sec")),
        P(),
        P(),
        P("sec", "ops", None, None),
        P(None, "ops", None, None),
    )
    return jax.shard_map(
        cube_shards, mesh=mesh, in_specs=placed, out_specs=P(("ops", "sec"), None, None), check_vma=False
    )
```

```python
import jax
import jax.numpy as jnp
from jax import lax
from jax.experimental import pallas as pl
from jax.experimental.pallas import tpu as pltpu
from jax.sharding import PartitionSpec as P

MESH = pl.DeviceIdType.MESH


def contract(running, packed, left_ids, right_ids, live_count, left_blocks, right_blocks):
    turn_count = (live_count + 1) // 2

    def advance(turn_index, current):
        first = 2 * turn_index
        block = lax.dynamic_slice_in_dim(packed, first, 2, 0)
        left_sel = lax.dynamic_slice_in_dim(left_ids, first, 2, 0)
        right_sel = lax.dynamic_slice_in_dim(right_ids, first, 2, 0)
        left_pick = left_blocks[left_sel]
        right_pick = right_blocks[right_sel]
        halfway = jnp.einsum("sij,stlj->stil", block, right_pick, precision=lax.Precision.HIGHEST)
        update = jnp.einsum("stmi,stil->sml", left_pick, halfway, precision=lax.Precision.HIGHEST)
        before = lax.dynamic_slice_in_dim(current, first, 2, 0)
        return lax.dynamic_update_slice_in_dim(current, before + update, first, 0)

    return lax.fori_loop(0, turn_count, advance, running)


def gather_whole(left_ops, right_ops):
    return (
        lax.all_gather(left_ops, "ops", axis=1, tiled=True),
        lax.all_gather(right_ops, "ops", axis=1, tiled=True),
    )


def arrange(incoming, tags, slot_count, width):
    incoming = incoming.reshape(slot_count, width, width)
    tag_ids = tags.reshape(slot_count).astype(jnp.int32)
    live_flag = (tag_ids > 0).astype(jnp.int32)
    order = jnp.argsort(1 - live_flag, stable=True)
    live_count = jnp.sum(live_flag)
    packed = incoming[order]
    right_ids = jnp.maximum(tag_ids[order] - 1, 0)
    return (packed, right_ids, order, live_count)


def shards(wavefunction, left_sector, right_sector, left_size, right_size, left_ops, right_ops):
    peer_count = lax.axis_size("sec")
    sec_local = left_ops.shape[0]
    width = wavefunction.shape[1]
    position = jnp.arange(width)
    left_live = jnp.sum(
        jnp.where(
            left_sector[:, None] == jnp.arange(left_size.shape[0])[None, :], left_size[None, :], 0
        ),
        axis=1,
    )
    right_live = jnp.sum(
        jnp.where(
            right_sector[:, None] == jnp.arange(right_size.shape[0])[None, :],
            right_size[None, :],
            0,
        ),
        axis=1,
    )
    row_live = position[None, :] < left_live[:, None]
    col_live = position[None, :] < right_live[:, None]
    window = (row_live[:, :, None] & col_live[:, None, :]).astype(jnp.float32)
    masked = wavefunction * window
    owner = left_sector // sec_local
    within = left_sector % sec_local
    outgoing = (
        jnp.zeros((peer_count, sec_local, width, width), jnp.float32).at[owner, within].set(masked)
    )
    labels = (
        jnp.zeros((peer_count, sec_local), jnp.float32)
        .at[owner, within]
        .set((right_sector + 1).astype(jnp.float32))
    )
    incoming, tags = (
        lax.all_to_all(outgoing, "sec", split_axis=0, concat_axis=0, tiled=True),
        lax.all_to_all(labels, "sec", split_axis=0, concat_axis=0, tiled=True),
    )
    slot_count = peer_count * sec_local
    packed, right_ids, order, live_count = arrange(incoming, tags, slot_count, width)
    left_ids = order % sec_local
    empty = jnp.zeros_like(packed)
    left_all, right_all = gather_whole(left_ops, right_ops)
    result = contract(empty, packed, left_ids, right_ids, live_count, left_all, right_all)
    restored = jnp.zeros_like(result).at[order].set(result)
    returned = lax.all_to_all(
        restored.reshape(peer_count, sec_local, width, width),
        "sec",
        split_axis=0,
        concat_axis=0,
        tiled=True,
    )
    return returned[owner, within] * window


def split(value):
    high = value.astype(jnp.bfloat16)
    low = (value - high.astype(jnp.float32)).astype(jnp.bfloat16)
    return high, low


LAND, SIBLING, ALONG_X, ALONG_Y, ALONG_UP, ALONG_DOWN, RIGHTS, LEFT, SIBLING_LEFT, LAND_SIBLING, FAR_END = range(11)

PROGRAMS = (
    (
        8, 308, 20, 220, 108, 600, 1, 201, 101, 610, 16, 301, 5, 704, 105, 716,
        305, 12, 120, 116, 900, 800, 41, 205, 916, 141, 28, 24, 112, 124, 901, 424,
        2, 202, 302, 428, 128, 816, 720, 601, 908, 17, 6, 206, 924, 306, 9, 611,
        804, 709, 712, 828, 705, 21, 109, 309, 13, 221, 700, 42, 142, 117, 801, 805,
        708, 102, 106, 10, 310, 3, 203, 121, 18, 113, 110, 602, 612, 22, 7, 207,
        307, 14, 118, 222, 909, 122, 917, 902, 722, 813, 706, 29, 107, 129, 103, 25,
        43, 303, 125, 918, 114, 143, 818, 821, 728, 820, 702, 717, 701, 724, 817, 824,
        721, 725, 808, 809, 806, 812, 713, 822, 26, 11, 603, 613, 710, 15, 23, 925,
        111, 910, 31, 903, 115, 126, 123, 814, 802, 703, 723, 731, 803, 131, 30, 19,
        119, 130, 27, 127, 911, 715, 719, 718, 707, 726, 815, 825, 727, 730, 829, 811,
        729, 711, 714, 810, 807, 919, 926, 927, 823, 831, 819, 827, 826, 830,
    ),
    (
        0, 300, 2, 200, 502, 202, 400, 6, 506, 306, 4, 304, 21, 601, 404, 102,
        104, 206, 106, 42, 142, 221, 542, 9, 611, 204, 13, 40, 709, 3, 109, 440,
        503, 302, 113, 602, 612, 103, 7, 16, 507, 702, 121, 17, 309, 203, 140, 303,
        107, 10, 14, 706, 24, 43, 143, 543, 424, 22, 307, 124, 8, 116, 207, 108,
        20, 100, 114, 600, 713, 28, 902, 29, 128, 110, 428, 310, 901, 120, 222, 117,
        610, 603, 613, 916, 720, 805, 714, 801, 721, 820, 11, 18, 12, 900, 717, 729,
        118, 910, 112, 15, 903, 115, 111, 31, 19, 924, 917, 718, 711, 816, 712, 908,
        812, 803, 25, 122, 119, 125, 30, 129, 909, 26, 716, 126, 23, 130, 817, 708,
        814, 809, 722, 821, 704, 918, 911, 27, 127, 123, 925, 131, 723, 730, 825, 710,
        715, 700, 707, 725, 806, 829, 813, 727, 724, 810, 800, 804, 926, 927, 919, 831,
        828, 703, 823, 808, 719, 827, 731, 830, 815, 818, 726, 705, 802, 811, 822, 826,
        819, 728, 807, 701, 824,
    ),
    (
        3, 203, 303, 503, 22, 1, 301, 602, 122, 222, 14, 401, 7, 507, 5, 10,
        405, 207, 18, 101, 612, 201, 305, 902, 43, 105, 143, 543, 806, 714, 103, 110,
        41, 307, 141, 118, 0, 400, 702, 205, 441, 603, 17, 11, 100, 4, 30, 310,
        19, 404, 601, 613, 200, 104, 300, 15, 304, 40, 119, 31, 21, 114, 531, 918,
        9, 440, 140, 121, 715, 204, 109, 111, 309, 818, 23, 901, 115, 27, 611, 26,
        221, 13, 24, 424, 8, 731, 113, 527, 600, 127, 124, 117, 108, 28, 16, 911,
        428, 128, 12, 909, 910, 112, 20, 107, 126, 900, 130, 131, 116, 610, 707, 719,
        701, 120, 924, 25, 917, 29, 129, 908, 927, 123, 125, 926, 720, 713, 817, 804,
        709, 810, 711, 703, 710, 718, 724, 723, 808, 801, 903, 916, 726, 827, 725, 830,
        717, 712, 729, 805, 828, 800, 728, 821, 813, 814, 815, 706, 705, 730, 727, 722,
        802, 824, 826, 811, 812, 803, 809, 919, 925, 716, 700, 721, 822, 831, 704, 820,
        708, 823, 819, 825, 829, 807, 816,
    ),
    (
        903, 603, 23, 223, 11, 311, 2, 302, 102, 613, 202, 707, 15, 6, 206, 123,
        111, 19, 42, 715, 803, 306, 703, 723, 31, 142, 27, 131, 115, 531, 106, 127,
        1, 301, 201, 527, 731, 727, 602, 711, 10, 5, 305, 110, 902, 205, 911, 612,
        310, 815, 22, 806, 0, 1031, 14, 101, 927, 200, 719, 1027, 18, 119, 105, 17,
        222, 9, 300, 109, 117, 811, 114, 41, 100, 141, 122, 118, 13, 113, 21, 121,
        807, 706, 4, 204, 304, 919, 601, 221, 26, 901, 909, 40, 140, 104, 8, 126,
        309, 917, 611, 701, 721, 805, 821, 726, 705, 30, 130, 900, 600, 819, 16, 918,
        24, 108, 124, 926, 822, 831, 910, 20, 12, 112, 120, 116, 610, 801, 823, 810,
        713, 720, 818, 702, 814, 29, 28, 25, 916, 908, 128, 125, 129, 718, 708, 717,
        813, 700, 802, 712, 812, 716, 714, 729, 725, 730, 820, 809, 724, 830, 817, 710,
        804, 827, 924, 925, 800, 826, 704, 829, 816, 808, 728, 722, 825, 828, 824, 709,
    ),
)


def gather_contract(
    wf_hbm, lops_hbm, rops_hbm, lsec_hbm, rsec_hbm, lsize_hbm, rsize_hbm,
    out_ref,
    wbuf, lbuf, rbuf, mcat, hcat, acc, lsec, rsec, lsize, rsize, inverse, right_of,
    own_sem, recv_own, recv_sib, recv_r, sends, entered,
):
    terms = lax.axis_size("ops")
    sectors, _, width, _ = lbuf.shape
    rights = rbuf.shape[1]
    half = width // 2
    z = lax.axis_index("ops")
    sec = lax.axis_index("sec")
    core = sec % 2
    xpos = (sec // 2) % 2
    ypos = sec // 4
    sib = sec + 1 - 2 * core
    xnb = sec + 2 - 4 * xpos
    ynb = sec + 4 - 8 * ypos
    dnb = xnb + 4 - 8 * ypos
    has_up = z < terms - 1
    has_dn = z > 0

    def flip(group):
        return group + 1 - 2 * core

    barrier = pltpu.get_barrier_semaphore()

    def greet(sem, zz, ss):
        pl.semaphore_signal(sem, inc=1, device_id=(zz, ss), device_id_type=MESH)

    links = (
        (xpos == 0, xpos == 1, z, xnb),
        (ypos == 0, ypos == 1, z, ynb),
        (has_up, has_dn, z, sec),
        (core == 1, core == 0, z, sib),
    )
    for k, (first, second, zz, ss) in enumerate(links):
        @pl.when(first)
        def _(k=k, zz=zz, ss=ss):
            greet(barrier, zz + 1 if k == 2 else zz, ss)

    scalar_in = [
        pltpu.make_async_copy(src, dst, own_sem.at[2 + n])
        for n, (src, dst) in enumerate(
            ((lsec_hbm, lsec), (rsec_hbm, rsec), (lsize_hbm, lsize), (rsize_hbm, rsize))
        )
    ]
    own_l = [
        pltpu.make_async_copy(lops_hbm.at[i, 0], lbuf.at[2 * sec + i, z], recv_own.at[0, i, z])
        for i in range(2)
    ]
    own_r = pltpu.make_async_copy(rops_hbm.at[:, 0], rbuf.at[z], own_sem.at[0])
    own_w = pltpu.make_async_copy(wf_hbm, wbuf, own_sem.at[1])
    for copy in scalar_in:
        copy.start()
    own_w.start()
    own_r.start()
    for copy in own_l:
        copy.start()
    firsts = xpos + ypos + has_dn.astype(jnp.int32) + 1 - core

    @pl.when(firsts > 0)
    def _():
        pl.semaphore_wait(barrier, firsts)

    for k, (first, second, zz, ss) in enumerate(links):
        @pl.when(second)
        def _(k=k, zz=zz, ss=ss):
            greet(entered.at[k], zz - 1 if k == 2 else zz, ss)

    def move(src, dst, ssem, rsem, zz, ss):
        return pltpu.make_async_remote_copy(
            src_ref=src, dst_ref=dst, send_sem=ssem, recv_sem=rsem,
            device_id=(zz, ss), device_id_type=MESH,
        )

    def piece(group, i, t, link, rsem, zz, ss, own=False):
        s = 2 * group + i
        src = lops_hbm.at[i, 0] if own else lbuf.at[s, t]
        return move(src, lbuf.at[s, t], sends.at[link], rsem, zz, ss)

    def rpiece(h, t, link, zz, ss, own=False):
        rows = pl.ds(pl.multiple_of(h * half, half), half)
        src = rops_hbm.at[:, 0, rows] if own else rbuf.at[t, :, rows]
        return move(src, rbuf.at[t, :, rows], sends.at[link], recv_r.at[t, h], zz, ss)

    def await_l(place, i, t):
        group = groups[place]
        piece(group, i, t, 0, recv_own.at[place, i, t], z, xnb).wait_recv()

    def await_pair(place, t):
        first = 2 * flip(groups[place])
        pair = lbuf.at[pl.ds(first, 2), t]
        move(pair, pair, sends.at[0], recv_sib.at[place, t], z, sib).wait_recv()

    def await_r(h, t):
        rpiece(h, t, 0, z, xnb).wait_recv()

    def drain(link, count):
        blocks = wbuf.at[pl.ds(0, count)]
        move(blocks, blocks, sends.at[link], recv_own.at[0, 0, 0], z, xnb).wait_send()

    groups = (sec, xnb, ynb, dnb)
    sides = {ALONG_UP: (2, 1), ALONG_DOWN: (3, -1)}

    def to_z(way, place, i, t, own=False):
        link, step = sides[way]
        return piece(groups[place], i, t, link, recv_own.at[place, i, t], z + step, sec, own)

    def to_far_end(place, i, t):
        return piece(groups[place], i, t, 3, recv_own.at[place, i, t], z + 1 - terms, sec)

    def right_z(way, t, own=False):
        link, step = sides[way]
        return rpiece(core, t, link, z + step, sec, own)

    def to_x(place, i, t, own=False):
        return piece(groups[place], i, t, 0, recv_own.at[place + 1, i, t], z, xnb, own)

    def to_y(place, i, t, own=False):
        return piece(groups[place], i, t, 1, recv_own.at[place + 2, i, t], z, ynb, own)

    def to_sib(place, i, t, own=False):
        link = 4 + (place + 1) // 2
        return piece(groups[place], i, t, link, recv_sib.at[place, t], z, sib, own)

    def own_z(way, own):
        return [to_z(way, 0, 0, z, own), to_z(way, 0, 1, z, own), right_z(way, z, own)]

    def own_sends(own):
        return (
            [to_x(0, 0, z, own), to_x(0, 1, z, own)],
            [to_y(0, 1, z, own), to_y(0, 0, z, own)],
            [to_sib(0, 0, z, own), to_sib(0, 1, z, own)],
        )

    def start(copies):
        for copy in copies:
            copy.start()

    @pl.when(xpos == 1)
    def _():
        start(own_sends(True)[0])

    @pl.when(ypos == 1)
    def _():
        start(own_sends(True)[1])

    @pl.when(has_dn)
    def _():
        start(own_z(ALONG_DOWN, True))

    @pl.when(core == 0)
    def _():
        start(own_sends(True)[2])

    for copy in scalar_in:
        copy.wait()
    for s in range(sectors):
        value = jnp.int32(0)
        for p in range(1, sectors):
            value = jnp.where(lsec[p] == s, p, value)
        inverse[s] = value
        right_of[s] = rsec[value]

    own_r.wait()
    for copy in own_l:
        copy.wait()

    @pl.when(core == 1)
    def _():
        pl.semaphore_wait(entered.at[3], 1)
        start(own_sends(False)[2])

    @pl.when(xpos == 0)
    def _():
        pl.semaphore_wait(entered.at[0], 1)
        start(own_sends(False)[0])

    @pl.when(ypos == 0)
    def _():
        pl.semaphore_wait(entered.at[1], 1)
        start(own_sends(False)[1])

    @pl.when(has_up)
    def _():
        pl.semaphore_wait(entered.at[2], 1)
        start(own_z(ALONG_UP, False))

    row_at = lax.broadcasted_iota(jnp.int32, (width, width), 0)
    col_at = lax.broadcasted_iota(jnp.int32, (width, width), 1)

    own_w.wait()

    @pl.loop(0, sectors)
    def _(s):
        live = (row_at < lsize[s]) & (col_at < rsize[right_of[s]])
        high, low_part = split(jnp.where(live, wbuf[inverse[s]], 0.0))
        rows = pl.ds(pl.multiple_of(s * width, width), width)
        mcat[rows, :width] = high
        mcat[rows, width:] = low_part
        acc[s] = jnp.zeros((width, width), jnp.float32)

    batch = sectors // 2

    def halfway(t, part):
        high, low_part = split(rbuf[t].reshape(rights * width, width))
        doubled = jnp.concatenate([high, high], axis=1)
        contract_last = (((1,), (1,)), ((), ()))
        left = mcat[part * batch * width : (part + 1) * batch * width, :]
        both = lax.dot_general(left, doubled, contract_last, preferred_element_type=jnp.float32)
        both += lax.dot_general(
            left[:, :width], low_part, contract_last, preferred_element_type=jnp.float32
        )
        for j in range(batch):
            s = part * batch + j
            mine = both[j * width : (j + 1) * width]
            which = jnp.full((width, width), right_of[s], jnp.int32)
            pick = mine[:, :width]
            for b in range(1, rights):
                pick = jnp.where(which == b, mine[:, b * width : (b + 1) * width], pick)
            h_high, h_low = split(pick)
            hcat[t, s, :, :width] = h_high
            hcat[t, s, :, width:] = h_low

    def apply_left(s, t):
        high, low_part = split(lbuf[s, t])
        wide = jnp.dot(
            jnp.concatenate([high, low_part], axis=0), hcat[t, s], preferred_element_type=jnp.float32
        )
        acc[s] += wide[:width, :width] + (wide[:width, width:] + wide[width:, :width])

    def run(program, here):
        count = [2, 2, 3 * (here < terms - 1), 3 * (here > 0), 2, 0, 0]

        def send(copy, link):
            copy.start()
            count[link] += 1

        for action in program:
            kind, operand = divmod(action, 100)
            link = {ALONG_X: 0, ALONG_Y: 1, ALONG_UP: 2, ALONG_DOWN: 3}.get(kind)
            if kind == RIGHTS:
                part, t = divmod(operand, 10)
                if t != here and part == 0:
                    await_r(1 - core, t)
                halfway(t, part)
                continue
            if operand >= 40:
                t = operand - 40
                if kind == LAND:
                    await_r(core, t)
                elif kind == SIBLING:
                    send(rpiece(core, t, 4, z, sib), 4)
                else:
                    send(right_z(kind, t), link)
                continue
            place, t = divmod(operand, 4)
            place, i = divmod(place, 2)
            if kind == LAND:
                await_l(place, i, t)
            elif kind == SIBLING:
                send(to_sib(place, i, t), 4 + (place + 1) // 2)
            elif kind == ALONG_X:
                send(to_x(place, i, t), link)
            elif kind == ALONG_Y:
                send(to_y(place, i, t), link)
            elif kind in sides:
                send(to_z(kind, place, i, t), link)
            elif kind == FAR_END:
                send(to_far_end(place, i, t), 3)
            elif kind == LEFT:
                apply_left(2 * groups[place] + i, t)
            elif kind == SIBLING_LEFT:
                apply_left(2 * flip(groups[place]) + i, t)
            else:
                await_pair(place, t)
        for link, copies in enumerate(count):
            if copies > 0:
                drain(link, copies)

    for here in range(terms):
        @pl.when(z == here)
        def _(here=here):
            run(PROGRAMS[here], here)

    for p in range(sectors):
        s = lsec[p]
        live = (row_at < lsize[s]) & (col_at < rsize[rsec[p]])
        out_ref[p] = jnp.where(live, acc[s], 0.0)


def local_shards(wavefunction, left_sector, right_sector, left_size, right_size, left_ops, right_ops):
    terms = lax.axis_size("ops")
    sectors, width = left_size.shape[0], wavefunction.shape[1]
    rights = right_size.shape[0]
    dma = pltpu.SemaphoreType.DMA
    operands = (
        wavefunction, left_ops, right_ops, left_sector, right_sector, left_size, right_size,
    )
    return pl.pallas_call(
        gather_contract,
        out_shape=pltpu.VMEM(wavefunction.shape, jnp.float32),
        in_specs=[pl.BlockSpec(memory_space=pltpu.HBM)] * 7,
        out_specs=pl.BlockSpec(memory_space=pltpu.VMEM),
        scratch_shapes=[
            pltpu.VMEM(wavefunction.shape, jnp.float32),
            pltpu.VMEM((sectors, terms, width, width), jnp.float32),
            pltpu.VMEM((terms, rights, width, width), jnp.float32),
            pltpu.VMEM((sectors * width, 2 * width), jnp.bfloat16),
            pltpu.VMEM((terms, sectors, width, 2 * width), jnp.bfloat16),
            pltpu.VMEM((sectors, width, width), jnp.float32),
            pltpu.SMEM(left_sector.shape, jnp.int32),
            pltpu.SMEM(right_sector.shape, jnp.int32),
            pltpu.SMEM(left_size.shape, jnp.int32),
            pltpu.SMEM(right_size.shape, jnp.int32),
            pltpu.SMEM((sectors,), jnp.int32),
            pltpu.SMEM((sectors,), jnp.int32),
            dma((6,)),
            dma((4, 2, terms)),
            dma((4, terms)),
            dma((terms, 2)),
            dma((7,)),
            pltpu.SemaphoreType.REGULAR((4,)),
        ],
        compiler_params=pltpu.CompilerParams(collective_id=0, has_side_effects=True, vmem_limit_bytes=40*2**20),
    )(*[pltpu.with_memory_space_constraint(array, pltpu.HBM) for array in operands])


def cube_shards(*arrays):
    wavefunction, left_size, left_ops = arrays[0], arrays[3], arrays[5]
    sectors, width = left_size.shape[0], wavefunction.shape[1]
    terms = lax.axis_size("ops")
    every_sector = wavefunction.shape[0] == sectors
    cube = lax.axis_size("sec") == 2**3 and terms == 2**2 and left_ops.shape[:2] == (2, 1)
    cube = cube and arrays[4].shape[0] == 2
    small = sectors * terms * width * width * 4 <= 2**23
    if every_sector and cube and small:
        return local_shards(*arrays)
    return shards(*arrays)


def solution(mesh):
    placed = (
        P(("ops", "sec"), None, None),
        P(("ops", "sec")),
        P(("ops", "sec")),
        P(),
        P(),
        P("sec", "ops", None, None),
        P(None, "ops", None, None),
    )
    return jax.shard_map(
        cube_shards, mesh=mesh, in_specs=placed, out_specs=P(("ops", "sec"), None, None), check_vma=False
    )
```

```python
import jax
import jax.numpy as jnp
from jax import lax
from jax.experimental import pallas as pl
from jax.experimental.pallas import tpu as pltpu
from jax.sharding import PartitionSpec as P

MESH = pl.DeviceIdType.MESH


def contract(running, packed, left_ids, right_ids, live_count, left_blocks, right_blocks):
    turn_count = (live_count + 1) // 2

    def advance(turn_index, current):
        first = 2 * turn_index
        block = lax.dynamic_slice_in_dim(packed, first, 2, 0)
        left_sel = lax.dynamic_slice_in_dim(left_ids, first, 2, 0)
        right_sel = lax.dynamic_slice_in_dim(right_ids, first, 2, 0)
        left_pick = left_blocks[left_sel]
        right_pick = right_blocks[right_sel]
        halfway = jnp.einsum("sij,stlj->stil", block, right_pick, precision=lax.Precision.HIGHEST)
        update = jnp.einsum("stmi,stil->sml", left_pick, halfway, precision=lax.Precision.HIGHEST)
        before = lax.dynamic_slice_in_dim(current, first, 2, 0)
        return lax.dynamic_update_slice_in_dim(current, before + update, first, 0)

    return lax.fori_loop(0, turn_count, advance, running)


def gather_whole(left_ops, right_ops):
    return (
        lax.all_gather(left_ops, "ops", axis=1, tiled=True),
        lax.all_gather(right_ops, "ops", axis=1, tiled=True),
    )


def arrange(incoming, tags, slot_count, width):
    incoming = incoming.reshape(slot_count, width, width)
    tag_ids = tags.reshape(slot_count).astype(jnp.int32)
    live_flag = (tag_ids > 0).astype(jnp.int32)
    order = jnp.argsort(1 - live_flag, stable=True)
    live_count = jnp.sum(live_flag)
    packed = incoming[order]
    right_ids = jnp.maximum(tag_ids[order] - 1, 0)
    return (packed, right_ids, order, live_count)


def shards(wavefunction, left_sector, right_sector, left_size, right_size, left_ops, right_ops):
    peer_count = lax.axis_size("sec")
    sec_local = left_ops.shape[0]
    width = wavefunction.shape[1]
    position = jnp.arange(width)
    left_live = jnp.sum(
        jnp.where(
            left_sector[:, None] == jnp.arange(left_size.shape[0])[None, :], left_size[None, :], 0
        ),
        axis=1,
    )
    right_live = jnp.sum(
        jnp.where(
            right_sector[:, None] == jnp.arange(right_size.shape[0])[None, :],
            right_size[None, :],
            0,
        ),
        axis=1,
    )
    row_live = position[None, :] < left_live[:, None]
    col_live = position[None, :] < right_live[:, None]
    window = (row_live[:, :, None] & col_live[:, None, :]).astype(jnp.float32)
    masked = wavefunction * window
    owner = left_sector // sec_local
    within = left_sector % sec_local
    outgoing = (
        jnp.zeros((peer_count, sec_local, width, width), jnp.float32).at[owner, within].set(masked)
    )
    labels = (
        jnp.zeros((peer_count, sec_local), jnp.float32)
        .at[owner, within]
        .set((right_sector + 1).astype(jnp.float32))
    )
    incoming, tags = (
        lax.all_to_all(outgoing, "sec", split_axis=0, concat_axis=0, tiled=True),
        lax.all_to_all(labels, "sec", split_axis=0, concat_axis=0, tiled=True),
    )
    slot_count = peer_count * sec_local
    packed, right_ids, order, live_count = arrange(incoming, tags, slot_count, width)
    left_ids = order % sec_local
    empty = jnp.zeros_like(packed)
    left_all, right_all = gather_whole(left_ops, right_ops)
    result = contract(empty, packed, left_ids, right_ids, live_count, left_all, right_all)
    restored = jnp.zeros_like(result).at[order].set(result)
    returned = lax.all_to_all(
        restored.reshape(peer_count, sec_local, width, width),
        "sec",
        split_axis=0,
        concat_axis=0,
        tiled=True,
    )
    return returned[owner, within] * window


def split(value):
    high = value.astype(jnp.bfloat16)
    low = (value - high.astype(jnp.float32)).astype(jnp.bfloat16)
    return high, low


LAND, SIBLING, ALONG_X, ALONG_Y, ALONG_UP, ALONG_DOWN, RIGHTS, LEFT, SIBLING_LEFT, LAND_SIBLING, FAR_END = range(11)

PROGRAMS = (
    (
        8, 308, 20, 220, 108, 600, 1, 201, 101, 610, 16, 301, 5, 704, 105, 716,
        305, 12, 120, 116, 900, 800, 41, 205, 916, 141, 28, 24, 112, 124, 901, 424,
        2, 202, 302, 428, 128, 816, 720, 601, 908, 17, 6, 206, 924, 306, 9, 611,
        804, 709, 712, 828, 705, 21, 109, 309, 13, 221, 700, 42, 142, 117, 801, 805,
        708, 102, 106, 10, 310, 3, 203, 121, 18, 113, 110, 602, 612, 22, 7, 207,
        307, 14, 118, 222, 909, 122, 917, 902, 722, 813, 706, 29, 107, 129, 103, 25,
        43, 303, 125, 918, 114, 143, 818, 821, 728, 820, 702, 717, 701, 724, 817, 824,
        721, 725, 808, 809, 806, 812, 713, 822, 26, 11, 603, 613, 710, 15, 23, 925,
        111, 910, 31, 903, 115, 126, 123, 814, 802, 703, 723, 731, 803, 131, 30, 19,
        119, 130, 27, 127, 911, 715, 719, 718, 707, 726, 815, 825, 727, 730, 829, 811,
        729, 711, 714, 810, 807, 919, 926, 927, 823, 831, 819, 827, 826, 830,
    ),
    (
        0, 300, 2, 200, 502, 202, 400, 6, 506, 306, 4, 304, 21, 601, 404, 102,
        104, 206, 106, 42, 142, 221, 542, 9, 611, 204, 13, 40, 709, 3, 109, 440,
        503, 302, 113, 602, 612, 103, 7, 16, 507, 702, 121, 17, 309, 203, 140, 303,
        107, 10, 14, 706, 24, 43, 143, 543, 424, 22, 307, 124, 8, 116, 207, 108,
        20, 100, 114, 600, 713, 28, 902, 29, 128, 110, 428, 310, 901, 120, 222, 117,
        610, 603, 613, 916, 720, 805, 714, 801, 721, 820, 11, 18, 12, 900, 717, 729,
        118, 910, 112, 15, 903, 115, 111, 31, 19, 924, 917, 718, 711, 816, 712, 908,
        812, 803, 25, 122, 119, 125, 30, 129, 909, 26, 716, 126, 23, 130, 817, 708,
        814, 809, 722, 821, 704, 918, 911, 27, 127, 123, 925, 131, 723, 730, 825, 710,
        715, 700, 707, 725, 806, 829, 813, 727, 724, 810, 800, 804, 926, 927, 919, 831,
        828, 703, 823, 808, 719, 827, 731, 830, 815, 818, 726, 705, 802, 811, 822, 826,
        819, 728, 807, 701, 824,
    ),
    (
        3, 203, 303, 503, 22, 1, 301, 602, 122, 222, 14, 401, 7, 507, 5, 10,
        405, 207, 18, 101, 612, 201, 305, 902, 43, 105, 143, 543, 806, 714, 103, 110,
        41, 307, 141, 118, 0, 400, 702, 205, 441, 603, 17, 11, 100, 4, 30, 310,
        19, 404, 601, 613, 200, 104, 300, 15, 304, 40, 119, 31, 21, 114, 531, 918,
        9, 440, 140, 121, 715, 204, 109, 111, 309, 818, 23, 901, 115, 27, 611, 26,
        221, 13, 24, 424, 8, 731, 113, 527, 600, 127, 124, 117, 108, 28, 16, 911,
        428, 128, 12, 909, 910, 112, 20, 107, 126, 900, 130, 131, 116, 610, 707, 719,
        701, 120, 924, 25, 917, 29, 129, 908, 927, 123, 125, 926, 720, 713, 817, 804,
        709, 810, 711, 703, 710, 718, 724, 723, 808, 801, 903, 916, 726, 827, 725, 830,
        717, 712, 729, 805, 828, 800, 728, 821, 813, 814, 815, 706, 705, 730, 727, 722,
        802, 824, 826, 811, 812, 803, 809, 919, 925, 716, 700, 721, 822, 831, 704, 820,
        708, 823, 819, 825, 829, 807, 816,
    ),
    (
        903, 603, 23, 223, 11, 311, 2, 302, 102, 613, 202, 707, 15, 6, 206, 123,
        111, 19, 42, 715, 803, 306, 703, 723, 31, 142, 27, 131, 115, 531, 106, 127,
        1, 301, 201, 527, 731, 727, 602, 711, 10, 5, 305, 110, 902, 205, 911, 612,
        310, 815, 22, 806, 0, 1031, 14, 101, 927, 200, 719, 1027, 18, 119, 105, 17,
        222, 9, 300, 109, 117, 811, 114, 41, 100, 141, 122, 118, 13, 113, 21, 121,
        807, 706, 4, 204, 304, 919, 601, 221, 26, 901, 909, 40, 140, 104, 8, 126,
        309, 917, 611, 701, 721, 805, 821, 726, 705, 30, 130, 900, 600, 819, 16, 918,
        24, 108, 124, 926, 822, 831, 910, 20, 12, 112, 120, 116, 610, 801, 823, 810,
        713, 720, 818, 702, 814, 29, 28, 25, 916, 908, 128, 125, 129, 718, 708, 717,
        813, 700, 802, 712, 812, 716, 714, 729, 725, 730, 820, 809, 724, 830, 817, 710,
        804, 827, 924, 925, 800, 826, 704, 829, 816, 808, 728, 722, 825, 828, 824, 709,
    ),
)


def gather_contract(
    wf_hbm, lops_hbm, rops_hbm, lsec_hbm, rsec_hbm, lsize_hbm, rsize_hbm,
    out_ref,
    wbuf, lbuf, rbuf, mcat, hcat, acc, lsec, rsec, lsize, rsize, inverse, right_of,
    own_sem, recv_own, recv_sib, recv_r, sends, entered,
):
    terms = lax.axis_size("ops")
    sectors, _, width, _ = lbuf.shape
    rights = rbuf.shape[1]
    half = width // 2
    z = lax.axis_index("ops")
    sec = lax.axis_index("sec")
    core = sec % 2
    xpos = (sec // 2) % 2
    ypos = sec // 4
    sib = sec + 1 - 2 * core
    xnb = sec + 2 - 4 * xpos
    ynb = sec + 4 - 8 * ypos
    dnb = xnb + 4 - 8 * ypos
    has_up = z < terms - 1
    has_dn = z > 0

    def flip(group):
        return group + 1 - 2 * core

    barrier = pltpu.get_barrier_semaphore()

    def greet(sem, zz, ss):
        pl.semaphore_signal(sem, inc=1, device_id=(zz, ss), device_id_type=MESH)

    links = (
        (xpos == 0, xpos == 1, z, xnb),
        (ypos == 0, ypos == 1, z, ynb),
        (has_up, has_dn, z, sec),
        (core == 1, core == 0, z, sib),
    )
    for k, (first, second, zz, ss) in enumerate(links):
        @pl.when(first)
        def _(k=k, zz=zz, ss=ss):
            greet(barrier, zz + 1 if k == 2 else zz, ss)

    scalar_in = [
        pltpu.make_async_copy(src, dst, own_sem.at[2 + n])
        for n, (src, dst) in enumerate(
            ((lsec_hbm, lsec), (rsec_hbm, rsec), (lsize_hbm, lsize), (rsize_hbm, rsize))
        )
    ]
    own_l = [
        pltpu.make_async_copy(lops_hbm.at[i, 0], lbuf.at[2 * sec + i, z], recv_own.at[0, i, z])
        for i in range(2)
    ]
    own_r = pltpu.make_async_copy(rops_hbm.at[:, 0], rbuf.at[z], own_sem.at[0])
    own_w = pltpu.make_async_copy(wf_hbm, wbuf, own_sem.at[1])
    for copy in scalar_in:
        copy.start()
    own_w.start()
    own_r.start()
    for copy in own_l:
        copy.start()
    firsts = xpos + ypos + has_dn.astype(jnp.int32) + 1 - core

    @pl.when(firsts > 0)
    def _():
        pl.semaphore_wait(barrier, firsts)

    for k, (first, second, zz, ss) in enumerate(links):
        @pl.when(second)
        def _(k=k, zz=zz, ss=ss):
            greet(entered.at[k], zz - 1 if k == 2 else zz, ss)

    def move(src, dst, ssem, rsem, zz, ss):
        return pltpu.make_async_remote_copy(
            src_ref=src, dst_ref=dst, send_sem=ssem, recv_sem=rsem,
            device_id=(zz, ss), device_id_type=MESH,
        )

    def piece(group, i, t, link, rsem, zz, ss, own=False):
        s = 2 * group + i
        src = lops_hbm.at[i, 0] if own else lbuf.at[s, t]
        return move(src, lbuf.at[s, t], sends.at[link], rsem, zz, ss)

    def rpiece(h, t, link, zz, ss, own=False):
        rows = pl.ds(pl.multiple_of(h * half, half), half)
        src = rops_hbm.at[:, 0, rows] if own else rbuf.at[t, :, rows]
        return move(src, rbuf.at[t, :, rows], sends.at[link], recv_r.at[t, h], zz, ss)

    def await_l(place, i, t):
        group = groups[place]
        piece(group, i, t, 0, recv_own.at[place, i, t], z, xnb).wait_recv()

    def await_pair(place, t):
        first = 2 * flip(groups[place])
        pair = lbuf.at[pl.ds(first, 2), t]
        move(pair, pair, sends.at[0], recv_sib.at[place, t], z, sib).wait_recv()

    def await_r(h, t):
        rpiece(h, t, 0, z, xnb).wait_recv()

    def drain(link, count):
        blocks = wbuf.at[pl.ds(0, count)]
        move(blocks, blocks, sends.at[link], recv_own.at[0, 0, 0], z, xnb).wait_send()

    groups = (sec, xnb, ynb, dnb)
    sides = {ALONG_UP: (2, 1), ALONG_DOWN: (3, -1)}

    def to_z(way, place, i, t, own=False):
        link, step = sides[way]
        return piece(groups[place], i, t, link, recv_own.at[place, i, t], z + step, sec, own)

    def to_far_end(place, i, t):
        return piece(groups[place], i, t, 3, recv_own.at[place, i, t], z + 1 - terms, sec)

    def right_z(way, t, own=False):
        link, step = sides[way]
        return rpiece(core, t, link, z + step, sec, own)

    def to_x(place, i, t, own=False):
        return piece(groups[place], i, t, 0, recv_own.at[place + 1, i, t], z, xnb, own)

    def to_y(place, i, t, own=False):
        return piece(groups[place], i, t, 1, recv_own.at[place + 2, i, t], z, ynb, own)

    def to_sib(place, i, t, own=False):
        link = 4 + (place + 1) // 2
        return piece(groups[place], i, t, link, recv_sib.at[place, t], z, sib, own)

    def own_z(way, own):
        return [to_z(way, 0, 0, z, own), to_z(way, 0, 1, z, own), right_z(way, z, own)]

    def own_sends(own):
        return (
            [to_x(0, 0, z, own), to_x(0, 1, z, own)],
            [to_y(0, 1, z, own), to_y(0, 0, z, own)],
            [to_sib(0, 0, z, own), to_sib(0, 1, z, own)],
        )

    def start(copies):
        for copy in copies:
            copy.start()

    @pl.when(xpos == 1)
    def _():
        start(own_sends(True)[0])

    @pl.when(ypos == 1)
    def _():
        start(own_sends(True)[1])

    @pl.when(has_dn)
    def _():
        start(own_z(ALONG_DOWN, True))

    @pl.when(core == 0)
    def _():
        start(own_sends(True)[2])

    own_r.wait()
    for copy in own_l:
        copy.wait()

    @pl.when(core == 1)
    def _():
        pl.semaphore_wait(entered.at[3], 1)
        start(own_sends(False)[2])

    @pl.when(xpos == 0)
    def _():
        pl.semaphore_wait(entered.at[0], 1)
        start(own_sends(False)[0])

    @pl.when(ypos == 0)
    def _():
        pl.semaphore_wait(entered.at[1], 1)
        start(own_sends(False)[1])

    @pl.when(has_up)
    def _():
        pl.semaphore_wait(entered.at[2], 1)
        start(own_z(ALONG_UP, False))

    for copy in scalar_in:
        copy.wait()
    for s in range(sectors):
        value = jnp.int32(0)
        for p in range(1, sectors):
            value = jnp.where(lsec[p] == s, p, value)
        inverse[s] = value
        right_of[s] = rsec[value]

    row_at = lax.broadcasted_iota(jnp.int32, (width, width), 0)
    col_at = lax.broadcasted_iota(jnp.int32, (width, width), 1)

    own_w.wait()

    @pl.loop(0, sectors)
    def _(s):
        live = (row_at < lsize[s]) & (col_at < rsize[right_of[s]])
        high, low_part = split(jnp.where(live, wbuf[inverse[s]], 0.0))
        rows = pl.ds(pl.multiple_of(s * width, width), width)
        mcat[rows, :width] = high
        mcat[rows, width:] = low_part
        acc[s] = jnp.zeros((width, width), jnp.float32)

    batch = sectors // 2

    def halfway(t, part):
        high, low_part = split(rbuf[t].reshape(rights * width, width))
        doubled = jnp.concatenate([high, high], axis=1)
        contract_last = (((1,), (1,)), ((), ()))
        left = mcat[part * batch * width : (part + 1) * batch * width, :]
        both = lax.dot_general(left, doubled, contract_last, preferred_element_type=jnp.float32)
        both += lax.dot_general(
            left[:, :width], low_part, contract_last, preferred_element_type=jnp.float32
        )
        for j in range(batch):
            s = part * batch + j
            mine = both[j * width : (j + 1) * width]
            which = jnp.full((width, width), right_of[s], jnp.int32)
            pick = mine[:, :width]
            for b in range(1, rights):
                pick = jnp.where(which == b, mine[:, b * width : (b + 1) * width], pick)
            h_high, h_low = split(pick)
            hcat[t, s, :, :width] = h_high
            hcat[t, s, :, width:] = h_low

    def apply_left(s, t):
        high, low_part = split(lbuf[s, t])
        wide = jnp.dot(
            jnp.concatenate([high, low_part], axis=0), hcat[t, s], preferred_element_type=jnp.float32
        )
        acc[s] += wide[:width, :width] + (wide[:width, width:] + wide[width:, :width])

    def run(program, here):
        count = [2, 2, 3 * (here < terms - 1), 3 * (here > 0), 2, 0, 0]

        def send(copy, link):
            copy.start()
            count[link] += 1

        for action in program:
            kind, operand = divmod(action, 100)
            link = {ALONG_X: 0, ALONG_Y: 1, ALONG_UP: 2, ALONG_DOWN: 3}.get(kind)
            if kind == RIGHTS:
                part, t = divmod(operand, 10)
                if t != here and part == 0:
                    await_r(1 - core, t)
                halfway(t, part)
                continue
            if operand >= 40:
                t = operand - 40
                if kind == LAND:
                    await_r(core, t)
                elif kind == SIBLING:
                    send(rpiece(core, t, 4, z, sib), 4)
                else:
                    send(right_z(kind, t), link)
                continue
            place, t = divmod(operand, 4)
            place, i = divmod(place, 2)
            if kind == LAND:
                await_l(place, i, t)
            elif kind == SIBLING:
                send(to_sib(place, i, t), 4 + (place + 1) // 2)
            elif kind == ALONG_X:
                send(to_x(place, i, t), link)
            elif kind == ALONG_Y:
                send(to_y(place, i, t), link)
            elif kind in sides:
                send(to_z(kind, place, i, t), link)
            elif kind == FAR_END:
                send(to_far_end(place, i, t), 3)
            elif kind == LEFT:
                apply_left(2 * groups[place] + i, t)
            elif kind == SIBLING_LEFT:
                apply_left(2 * flip(groups[place]) + i, t)
            else:
                await_pair(place, t)
        for link, copies in enumerate(count):
            if copies > 0:
                drain(link, copies)

    for here in range(terms):
        @pl.when(z == here)
        def _(here=here):
            run(PROGRAMS[here], here)

    for p in range(sectors):
        s = lsec[p]
        live = (row_at < lsize[s]) & (col_at < rsize[rsec[p]])
        out_ref[p] = jnp.where(live, acc[s], 0.0)


def local_shards(wavefunction, left_sector, right_sector, left_size, right_size, left_ops, right_ops):
    terms = lax.axis_size("ops")
    sectors, width = left_size.shape[0], wavefunction.shape[1]
    rights = right_size.shape[0]
    dma = pltpu.SemaphoreType.DMA
    operands = (
        wavefunction, left_ops, right_ops, left_sector, right_sector, left_size, right_size,
    )
    return pl.pallas_call(
        gather_contract,
        out_shape=pltpu.VMEM(wavefunction.shape, jnp.float32),
        in_specs=[pl.BlockSpec(memory_space=pltpu.HBM)] * 7,
        out_specs=pl.BlockSpec(memory_space=pltpu.VMEM),
        scratch_shapes=[
            pltpu.VMEM(wavefunction.shape, jnp.float32),
            pltpu.VMEM((sectors, terms, width, width), jnp.float32),
            pltpu.VMEM((terms, rights, width, width), jnp.float32),
            pltpu.VMEM((sectors * width, 2 * width), jnp.bfloat16),
            pltpu.VMEM((terms, sectors, width, 2 * width), jnp.bfloat16),
            pltpu.VMEM((sectors, width, width), jnp.float32),
            pltpu.SMEM(left_sector.shape, jnp.int32),
            pltpu.SMEM(right_sector.shape, jnp.int32),
            pltpu.SMEM(left_size.shape, jnp.int32),
            pltpu.SMEM(right_size.shape, jnp.int32),
            pltpu.SMEM((sectors,), jnp.int32),
            pltpu.SMEM((sectors,), jnp.int32),
            dma((6,)),
            dma((4, 2, terms)),
            dma((4, terms)),
            dma((terms, 2)),
            dma((7,)),
            pltpu.SemaphoreType.REGULAR((4,)),
        ],
        compiler_params=pltpu.CompilerParams(collective_id=0, has_side_effects=True, vmem_limit_bytes=40*2**20),
    )(*[pltpu.with_memory_space_constraint(array, pltpu.HBM) for array in operands])


def cube_shards(*arrays):
    wavefunction, left_size, left_ops = arrays[0], arrays[3], arrays[5]
    sectors, width = left_size.shape[0], wavefunction.shape[1]
    terms = lax.axis_size("ops")
    every_sector = wavefunction.shape[0] == sectors
    cube = lax.axis_size("sec") == 2**3 and terms == 2**2 and left_ops.shape[:2] == (2, 1)
    cube = cube and arrays[4].shape[0] == 2
    small = sectors * terms * width * width * 4 <= 2**23
    if every_sector and cube and small:
        return local_shards(*arrays)
    return shards(*arrays)


def solution(mesh):
    placed = (
        P(("ops", "sec"), None, None),
        P(("ops", "sec")),
        P(("ops", "sec")),
        P(),
        P(),
        P("sec", "ops", None, None),
        P(None, "ops", None, None),
    )
    return jax.shard_map(
        cube_shards, mesh=mesh, in_specs=placed, out_specs=P(("ops", "sec"), None, None), check_vma=False
    )
```
